32 devices in a mesh: dp: 16 (over z, x, core), rep: 2 (over y).
Axes of the slice: x: 2, y: 2, z: 4, core: 2. Of those that a mesh axis runs over, the one named last changes fastest.
Arguments:
- grad_out: bfloat16 [12288, 2048], P('dp', 'rep'), may hold values from -6 to 6
- pre_act: bfloat16 [12288, 3072], P('dp', 'rep'), may hold values from -6 to 6
- up_weight: bfloat16 [3072, 2048], P('rep'), may hold values from -0.125 to 0.125
- down_weight: bfloat16 [2048, 3072], P(None, 'rep'), may hold values from -0.109375 to 0.109375
- slot_counts: int32 [16], P('dp'), may hold values from 384 to 768, as said below
Outputs:
- input_grad: bfloat16 [12288, 2048], P('dp')
- down_grad: float32 [2048, 3072], P('dp', 'rep')
The draws below stay inside these ranges and needn't reach their ends.
Inputs may be any that keep to these rules, and one draw needn't show every extreme that they name: Row i * 768 + j is live exactly when j < slot_counts[i]; some index has all 768 slots live and some index exactly 384.
All inputs are finite; a program needn't handle non-finite values.
Results may differ from the reference program's by a relative error of at most 0.0049.
Values may be sent and summed in bfloat16 or wider, within the bound.
A program may use at most 128 MiB of HBM per device.

```python
import jax
import jax.numpy as jnp
from jax import lax

D = 2048
FF = 3072
CAP = 768
ROWS = 12288
N_DP = 16


def draw_slot_counts(key, part):
    counts = jax.random.randint(key, (N_DP,), CAP // 2, CAP + 1)
    fullest = jax.random.randint(jax.random.fold_in(key, 1), (), 0, N_DP)
    step_away = jax.random.randint(jax.random.fold_in(key, 2), (), 1, max(N_DP, 2))
    emptiest = (fullest + step_away) % N_DP
    counts = counts.at[emptiest].set(CAP // 2)
    counts = counts.at[fullest].set(CAP)
    return counts.astype(jnp.int32)


def with_spikes(values, rng, source, target, shards_of, factor):
    def block_of(axis_at):
        return (jnp.arange(values.shape[axis_at]) // (values.shape[axis_at] // shards_of)).reshape((-1,) + (1,) * (values.ndim - 1 - axis_at))

    near = jax.random.permutation(rng, shards_of)[block_of(target)]
    other_side = (block_of(target) + shards_of // 2) % shards_of
    return jnp.where((block_of(source) == near) | (block_of(source) == other_side), factor * values, values)


def shard_levels(key, shape, cuts, smallest, high):
    def one(axis_at, parts):
        heights = jax.random.uniform(jax.random.fold_in(jax.random.fold_in(key, 6), axis_at), (parts,), jnp.float32, smallest / len(cuts), high / len(cuts))
        return jnp.repeat(jnp.exp(heights), shape[axis_at] // parts).reshape((-1,) + (1,) * (len(shape) - axis_at - 1))

    loudness = one(*cuts[0])
    for cut in cuts[1:]:
        loudness = loudness * one(*cut)
    return loudness


def normal_values(own_key, shape, deviation, most, cuts=(), kind=jnp.bfloat16):
    drawn = deviation * jax.random.normal(own_key, shape, jnp.float32)
    if cuts:
        drawn = drawn * shard_levels(own_key, shape, cuts, -0.22, 0.18)
    return jnp.clip(drawn, -most, most).astype(kind)


def noise_with(own_key, extent, width, limit, shards, heavy, dtype=jnp.bfloat16):
    entries = width * jax.random.normal(own_key, extent, jnp.float32)
    if shards:
        entries = entries * shard_levels(own_key, extent, shards, -0.22, 0.18)
    return jnp.clip(with_spikes(entries, jax.random.fold_in(own_key, 3), *heavy), -limit, limit).astype(dtype)


def setup_inputs(seed: int = 0) -> dict:
    splits = jax.random.split(jax.random.key(seed), 6)
    grad_out = noise_with(splits[0], (ROWS, D), 1.0, 6.0, ((0, 16), (1, 2)), (0, 1, 16, 2.0))
    pre_act = normal_values(splits[1], (ROWS, FF), 1.0, 6.0, ((0, 16), (1, 2)))
    up_weight = normal_values(splits[2], (FF, D), D ** -0.5, 0.125, ((0, 2),))
    down_weight = normal_values(splits[3], (D, FF), FF ** -0.5, 0.109375, ((1, 2),))
    slot_counts = draw_slot_counts(jax.random.fold_in(splits[5], 71), 0)
    return {"grad_out": grad_out, "pre_act": pre_act, "up_weight": up_weight, "down_weight": down_weight, "slot_counts": slot_counts}


def reference(grad_out, pre_act, up_weight, down_weight, slot_counts):
    row_index = lax.iota(jnp.int32, N_DP * CAP)
    live_rows = ((row_index % CAP) < slot_counts[row_index // CAP])[:, None]
    grad_live = jnp.where(live_rows, grad_out, jnp.zeros_like(grad_out))
    zero_pre = jnp.zeros_like(pre_act)
    hidden = jnp.where(live_rows, jnp.maximum(pre_act, zero_pre), zero_pre)
    down_grad = jnp.dot(grad_live.T, hidden, preferred_element_type=jnp.float32) / N_DP
    hidden_grad = jnp.dot(grad_live, down_weight, preferred_element_type=jnp.float32)
    pre_grad = jnp.where(pre_act > 0, hidden_grad, jnp.zeros_like(hidden_grad)).astype(jnp.bfloat16)
    input_grad = jnp.dot(pre_grad, up_weight, preferred_element_type=jnp.float32).astype(jnp.bfloat16)
    return input_grad, down_grad
```

```python
import functools

import jax
import jax.numpy as jnp
from jax import lax
from jax.experimental import pallas as pl
from jax.experimental.pallas import tpu as pltpu
from jax.sharding import PartitionSpec as P

MESH = pl.DeviceIdType.MESH
CHUNK = 128


def tile_of(extent):
    return next(t for t in (512, 384, 256, 128) if extent % t == 0)


def kernel(n_dp, n_rep, counts, grad, pre, up, down, ig_out, dg_out,
           gfull, pre_v, hid, up_v, down_v, terms, from_core, from_x, from_z, part, obuf, pg, dg_v,
           load_sem, g_send, g_recv, p_send, p_recv, c_send, c_recv, x_send, x_recv, z_send, z_recv,
           out_sem, dg_sem):
    rows, d_own = grad.shape
    ff = pre.shape[1]
    d_all = down.shape[0]
    n_z = n_dp // 4
    z_own = n_z // n_rep
    blk = d_all // n_dp
    n_chunks = rows // CHUNK
    ff_tile, d_tile = tile_of(ff), tile_of(d_all)

    me = lax.axis_index("dp")
    rep = lax.axis_index("rep")
    my_z, my_x, my_c = me // 4, (me // 2) % 2, me % 2
    core_peer = {"dp": my_z * 4 + my_x * 2 + (1 - my_c)}
    x_peer = {"dp": my_z * 4 + (1 - my_x) * 2 + my_c}
    rep_peers = [lax.rem(rep + o, n_rep) for o in range(1, n_rep)]

    def z_peer(z):
        return {"dp": z * 4 + my_x * 2 + my_c}

    loads = [
        pltpu.make_async_copy(src, dst, load_sem.at[i])
        for i, (src, dst) in enumerate(
            ((grad, gfull.at[rep]), (pre, pre_v), (down, down_v), (up, up_v)))
    ]
    for load in loads:
        load.start()

    barrier = pltpu.get_barrier_semaphore()
    peers = [{"rep": r} for r in rep_peers] + [core_peer, x_peer]
    peers += [z_peer(lax.rem(my_z + o, n_z)) for o in range(1, n_z)]
    for peer in peers:
        pl.semaphore_signal(barrier, inc=1, device_id=peer, device_id_type=MESH)
    pl.semaphore_wait(barrier, len(peers))

    def rows_of(c):
        return pl.ds(pl.multiple_of(c * CHUNK, CHUNK), CHUNK)

    def grad_copy(c, o, source):
        return pltpu.make_async_remote_copy(
            src_ref=grad.at[rows_of(c)], dst_ref=gfull.at[source, rows_of(c)],
            send_sem=g_send.at[c, o], recv_sem=g_recv.at[c, source],
            device_id={"rep": lax.rem(rep + o, n_rep)}, device_id_type=MESH)

    def part_copy(c, o, source):
        return pltpu.make_async_remote_copy(
            src_ref=part.at[rep, rows_of(c)], dst_ref=part.at[source, rows_of(c)],
            send_sem=p_send.at[c, o], recv_sem=p_recv.at[c, source],
            device_id={"rep": lax.rem(rep + o, n_rep)}, device_id_type=MESH)

    for c in range(n_chunks):
        for o in range(1, n_rep):
            grad_copy(c, o, rep).start()

    loads[1].wait()
    count = counts[0]

    def mask_rows(c, _):
        at = lax.broadcasted_iota(jnp.int32, (CHUNK, ff), 0) + c * CHUNK
        kept = jnp.where(at < count, pre_v[rows_of(c), :].astype(jnp.float32), 0.0)
        kept = jnp.maximum(kept, 0.0)
        hid[rows_of(c), :] = kept.astype(jnp.bfloat16)
        return 0

    lax.fori_loop(0, n_chunks, mask_rows, 0)
    loads[0].wait()

    def core_copy(z):
        return pltpu.make_async_remote_copy(
            src_ref=terms.at[z, 1 - my_c], dst_ref=from_core.at[z],
            send_sem=c_send.at[z], recv_sem=c_recv.at[z],
            device_id=core_peer, device_id_type=MESH)

    def x_copy(z):
        return pltpu.make_async_remote_copy(
            src_ref=from_core.at[z, 1 - my_x], dst_ref=from_x.at[z],
            send_sem=x_send.at[z], recv_sem=x_recv.at[z],
            device_id=x_peer, device_id_type=MESH)

    def z_copy(z, source):
        return pltpu.make_async_remote_copy(
            src_ref=from_x.at[z], dst_ref=from_z.at[source],
            send_sem=z_send.at[z], recv_sem=z_recv.at[source],
            device_id=z_peer(z), device_id_type=MESH)

    def z_at(k):
        return lax.rem(rep * z_own + k, n_z)

    def make_terms(k, _):
        z = z_at(k)
        group = z // z_own
        cols = pl.ds(pl.multiple_of((z - group * z_own) * 4 * blk, 4 * blk), 4 * blk)

        def one(j, _):
            at = pl.ds(pl.multiple_of(j * ff_tile, ff_tile), ff_tile)
            out = lax.dot_general(
                gfull[group, :, cols], hid[:, at], (((0,), (0,)), ((), ())),
                preferred_element_type=jnp.float32).astype(jnp.bfloat16)
            for x in range(2):
                for core in range(2):
                    row = (x * 2 + core) * blk
                    terms[z, core, x, :, at] = out[row:row + blk]
            return 0

        lax.fori_loop(0, ff // ff_tile, one, 0)
        core_copy(z).start()
        return 0

    def add_core(k, _):
        z = z_at(k)
        core_copy(z).wait()
        for x in range(2):
            total = from_core[z, x].astype(jnp.float32) + terms[z, my_c, x].astype(jnp.float32)
            from_core[z, x] = total.astype(jnp.bfloat16)
        x_copy(z).start()
        return 0

    def add_x(k, _):
        z = z_at(k)
        x_copy(z).wait()
        total = from_x[z].astype(jnp.float32) + from_core[z, my_x].astype(jnp.float32)
        from_x[z] = total.astype(jnp.bfloat16)

        @pl.when(z != my_z)
        def _():
            z_copy(z, my_z).start()

        return 0

    def chunk(c, _):
        at_rows = rows_of(c)
        for o in range(1, n_rep):
            grad_copy(c, o, lax.rem(rep + o, n_rep)).wait_recv()

        def hidden_tile(j, _):
            at = pl.ds(pl.multiple_of(j * ff_tile, ff_tile), ff_tile)
            total = jnp.dot(gfull[0, at_rows, :], down_v[:d_own, at],
                            preferred_element_type=jnp.float32)
            for g in range(1, n_rep):
                total += jnp.dot(gfull[g, at_rows, :], down_v[g * d_own:(g + 1) * d_own, at],
                                 preferred_element_type=jnp.float32)
            passed = hid[at_rows, at].astype(jnp.float32) > 0.0
            pg[:, at] = jnp.where(passed, total, 0.0).astype(jnp.bfloat16)
            return 0

        lax.fori_loop(0, ff // ff_tile, hidden_tile, 0)

        def out_tile(j, _):
            at = pl.ds(pl.multiple_of(j * d_tile, d_tile), d_tile)
            part[rep, at_rows, at] = jnp.dot(
                pg[...], up_v[:, at], preferred_element_type=jnp.float32).astype(jnp.bfloat16)
            return 0

        lax.fori_loop(0, d_all // d_tile, out_tile, 0)
        for o in range(1, n_rep):
            part_copy(c, o, rep).start()
        return 0

    lax.fori_loop(0, z_own, make_terms, 0)
    loads[2].wait()
    loads[3].wait()
    third = max(n_chunks // 3, 1)
    lax.fori_loop(0, third, chunk, 0)
    lax.fori_loop(0, z_own, add_core, 0)
    lax.fori_loop(third, 2 * third, chunk, 0)
    lax.fori_loop(0, z_own, add_x, 0)
    lax.fori_loop(2 * third, n_chunks, chunk, 0)
    lax.fori_loop(z_own, n_z, make_terms, 0)
    lax.fori_loop(z_own, n_z, add_core, 0)
    lax.fori_loop(z_own, n_z, add_x, 0)

    def out_copy(c):
        return pltpu.make_async_copy(obuf.at[rows_of(c)], ig_out.at[rows_of(c)], out_sem.at[c])

    def finish(c, _):
        at_rows = rows_of(c)
        for o in range(1, n_rep):
            part_copy(c, o, lax.rem(rep + o, n_rep)).wait_recv()
        total = part[0, at_rows, :].astype(jnp.float32)
        for g in range(1, n_rep):
            total += part[g, at_rows, :].astype(jnp.float32)
        obuf[at_rows, :] = total.astype(jnp.bfloat16)
        out_copy(c).start()
        return 0

    lax.fori_loop(0, n_chunks // 2, finish, 0)

    total = from_x[my_z].astype(jnp.float32)
    for o in range(1, n_z):
        source = lax.rem(my_z + o, n_z)
        z_copy(source, source).wait()
        total += from_z[source].astype(jnp.float32)
    dg_v[...] = total / n_dp
    dg_copy = pltpu.make_async_copy(dg_v, dg_out, dg_sem)
    dg_copy.start()

    lax.fori_loop(n_chunks // 2, n_chunks, finish, 0)
    for c in range(n_chunks):
        for o in range(1, n_rep):
            grad_copy(c, o, rep).wait_send()
            part_copy(c, o, rep).wait_send()
        out_copy(c).wait()
    dg_copy.wait()


def on_device(n_dp, n_rep, grad_out, pre_act, up_weight, down_weight, slot_counts):
    rows, d_own = grad_out.shape
    ff = pre_act.shape[1]
    d_all = down_weight.shape[0]
    n_z = n_dp // 4
    blk = d_all // n_dp
    n_chunks = rows // CHUNK
    any_ref = pl.BlockSpec(memory_space=pl.ANY)
    bf16, dma = jnp.bfloat16, pltpu.SemaphoreType.DMA
    return pl.pallas_call(
        functools.partial(kernel, n_dp, n_rep),
        out_shape=(jax.ShapeDtypeStruct((rows, d_all), bf16),
                   jax.ShapeDtypeStruct((blk, ff), jnp.float32)),
        in_specs=[pl.BlockSpec(memory_space=pltpu.SMEM)] + [any_ref] * 4,
        out_specs=(any_ref, any_ref),
        scratch_shapes=[
            pltpu.VMEM((n_rep, rows, d_own), bf16),
            pltpu.VMEM((rows, ff), bf16),
            pltpu.VMEM((rows, ff), bf16),
            pltpu.VMEM((ff, d_all), bf16),
            pltpu.VMEM((d_all, ff), bf16),
            pltpu.VMEM((n_z, 2, 2, blk, ff), bf16),
            pltpu.VMEM((n_z, 2, blk, ff), bf16),
            pltpu.VMEM((n_z, blk, ff), bf16),
            pltpu.VMEM((n_z, blk, ff), bf16),
            pltpu.VMEM((n_rep, rows, d_all), bf16),
            pltpu.VMEM((rows, d_all), bf16),
            pltpu.VMEM((CHUNK, ff), bf16),
            pltpu.VMEM((blk, ff), jnp.float32),
            dma((4,)),
            dma((n_chunks, n_rep)), dma((n_chunks, n_rep)),
            dma((n_chunks, n_rep)), dma((n_chunks, n_rep)),
            dma((n_z,)), dma((n_z,)), dma((n_z,)), dma((n_z,)), dma((n_z,)), dma((n_z,)),
            dma((n_chunks,)), dma,
        ],
        compiler_params=pltpu.CompilerParams(
            collective_id=0, has_side_effects=True, vmem_limit_bytes=63 * 2**20),
    )(slot_counts, grad_out, pre_act, up_weight, down_weight)


def solution(mesh):
    sizes = dict(mesh.shape)
    return jax.shard_map(
        functools.partial(on_device, sizes["dp"], sizes["rep"]),
        mesh=mesh,
        in_specs=(P("dp", "rep"), P("dp", "rep"), P("rep", None), P(None, "rep"), P("dp")),
        out_specs=(P("dp", None), P("dp", "rep")),
        check_vma=False,
    )
```

```python
import functools

import jax
import jax.numpy as jnp
from jax import lax
from jax.experimental import pallas as pl
from jax.experimental.pallas import tpu as pltpu
from jax.sharding import PartitionSpec as P

MESH = pl.DeviceIdType.MESH
CHUNK = 128


def tile_of(extent):
    return next(t for t in (512, 384, 256, 128) if extent % t == 0)


def kernel(n_dp, n_rep, counts, grad, pre, up, down, ig_out, dg_out,
           gfull, pre_v, hid, up_all, down_v, terms, from_core, from_x, from_z, masked, own_sum, other_sum, obuf, dg_v,
           load_sem, g_send, g_recv, p_send, p_recv, uy_send, u_send, u_recv, c_send, c_recv, x_send, x_recv, z_send, z_recv,
           out_sem, dg_sem):
    rows, d_own = grad.shape
    ff = pre.shape[1]
    d_all = down.shape[0]
    n_z = n_dp // 4
    z_own = n_z // n_rep
    blk = d_all // n_dp
    n_chunks = rows // CHUNK
    ff_tile, d_tile = tile_of(ff), tile_of(d_all)
    slice_rows = n_dp
    while ff % (slice_rows * 16):
        slice_rows //= 2
    slice_cols = n_dp // slice_rows
    tall, wide = ff // slice_rows, d_all // slice_cols

    me = lax.axis_index("dp")
    rep = lax.axis_index("rep")
    my_z, my_x, my_c = me // 4, (me // 2) % 2, me % 2
    core_peer = {"dp": my_z * 4 + my_x * 2 + (1 - my_c)}
    x_peer = {"dp": my_z * 4 + (1 - my_x) * 2 + my_c}
    rep_peers = [lax.rem(rep + o, n_rep) for o in range(1, n_rep)]

    def z_peer(z):
        return {"dp": z * 4 + my_x * 2 + my_c}

    loads = [
        pltpu.make_async_copy(src, dst, load_sem.at[i])
        for i, (src, dst) in enumerate(
            ((grad, gfull.at[rep]), (pre, pre_v), (down, down_v), (up, up_all.at[rep])))
    ]
    for load in loads:
        load.start()

    barrier = pltpu.get_barrier_semaphore()
    peers = [{"rep": r} for r in rep_peers] + [core_peer, x_peer]
    peers += [z_peer(lax.rem(my_z + o, n_z)) for o in range(1, n_z)]
    for peer in peers:
        pl.semaphore_signal(barrier, inc=1, device_id=peer, device_id_type=MESH)
    pl.semaphore_wait(barrier, len(peers))

    def rows_of(c):
        return pl.ds(pl.multiple_of(c * CHUNK, CHUNK), CHUNK)

    def grad_copy(c, o, source):
        return pltpu.make_async_remote_copy(
            src_ref=grad.at[rows_of(c)], dst_ref=gfull.at[source, rows_of(c)],
            send_sem=g_send.at[c, o], recv_sem=g_recv.at[c, source],
            device_id={"rep": lax.rem(rep + o, n_rep)}, device_id_type=MESH)

    def part_copy(c, o, source):
        return pltpu.make_async_remote_copy(
            src_ref=masked.at[rep, rows_of(c)], dst_ref=masked.at[source, rows_of(c)],
            send_sem=p_send.at[c, o], recv_sem=p_recv.at[c, source],
            device_id={"rep": lax.rem(rep + o, n_rep)}, device_id_type=MESH)

    def slice_at(s):
        down_at = pl.ds(pl.multiple_of((s // slice_cols) * tall, tall), tall)
        if slice_cols == 1:
            return (down_at,)
        return (down_at, pl.ds(pl.multiple_of((s % slice_cols) * wide, wide), wide))

    def up_rep_copy(o, source):
        return pltpu.make_async_remote_copy(
            src_ref=up.at[slice_at(me)], dst_ref=up_all.at[(source,) + slice_at(me)],
            send_sem=uy_send.at[o], recv_sem=u_recv.at[source, me],
            device_id={"rep": lax.rem(rep + o, n_rep)}, device_id_type=MESH)

    def up_copy(g, s, stage, peer):
        block = up_all.at[(g,) + slice_at(s)]
        return pltpu.make_async_remote_copy(
            src_ref=block, dst_ref=block, send_sem=u_send.at[g, stage], recv_sem=u_recv.at[g, s],
            device_id=peer, device_id_type=MESH)

    def index_of(z, x, core):
        return z * 4 + x * 2 + core

    def over_z(g, z):
        return up_copy(g, me, z, z_peer(z))

    def over_x(g, z):
        return up_copy(g, index_of(z, my_x, my_c), n_z + z, x_peer)

    def over_core(g, z, x):
        return up_copy(g, index_of(z, x, my_c), 2 * n_z + 2 * z + x, core_peer)

    def landed(g, s):
        up_copy(g, s, 0, core_peer).wait_recv()

    for o in range(1, n_rep):
        up_rep_copy(o, rep).start()
    for c in range(n_chunks):
        for o in range(1, n_rep):
            grad_copy(c, o, rep).start()

    loads[1].wait()
    count = counts[0]

    def mask_rows(c, _):
        at = lax.broadcasted_iota(jnp.int32, (CHUNK, ff), 0) + c * CHUNK
        kept = jnp.where(at < count, pre_v[rows_of(c), :].astype(jnp.float32), 0.0)
        kept = jnp.maximum(kept, 0.0)
        hid[rows_of(c), :] = kept.astype(jnp.bfloat16)
        return 0

    lax.fori_loop(0, n_chunks, mask_rows, 0)
    loads[0].wait()

    def core_copy(z):
        return pltpu.make_async_remote_copy(
            src_ref=terms.at[z, 1 - my_c], dst_ref=from_core.at[z],
            send_sem=c_send.at[z], recv_sem=c_recv.at[z],
            device_id=core_peer, device_id_type=MESH)

    def x_copy(z):
        return pltpu.make_async_remote_copy(
            src_ref=from_core.at[z, 1 - my_x], dst_ref=from_x.at[z],
            send_sem=x_send.at[z], recv_sem=x_recv.at[z],
            device_id=x_peer, device_id_type=MESH)

    def z_copy(z, source):
        return pltpu.make_async_remote_copy(
            src_ref=from_x.at[z], dst_ref=from_z.at[source],
            send_sem=z_send.at[z], recv_sem=z_recv.at[source],
            device_id=z_peer(z), device_id_type=MESH)

    def z_at(k):
        return lax.rem(rep * z_own + k, n_z)

    def make_terms(k, _):
        z = z_at(k)
        group = z // z_own
        cols = pl.ds(pl.multiple_of((z - group * z_own) * 4 * blk, 4 * blk), 4 * blk)

        def one(j, _):
            at = pl.ds(pl.multiple_of(j * ff_tile, ff_tile), ff_tile)
            out = lax.dot_general(
                gfull[group, :, cols], hid[:, at], (((0,), (0,)), ((), ())),
                preferred_element_type=jnp.float32).astype(jnp.bfloat16)
            for x in range(2):
                for core in range(2):
                    row = (x * 2 + core) * blk
                    terms[z, core, x, :, at] = out[row:row + blk]
            return 0

        lax.fori_loop(0, ff // ff_tile, one, 0)
        core_copy(z).start()
        return 0

    def add_core(k, _):
        z = z_at(k)
        core_copy(z).wait()
        for x in range(2):
            total = from_core[z, x].astype(jnp.float32) + terms[z, my_c, x].astype(jnp.float32)
            from_core[z, x] = total.astype(jnp.bfloat16)
        x_copy(z).start()
        return 0

    def add_x(k, _):
        z = z_at(k)
        x_copy(z).wait()
        total = from_x[z].astype(jnp.float32) + from_core[z, my_x].astype(jnp.float32)
        from_x[z] = total.astype(jnp.bfloat16)

        @pl.when(z != my_z)
        def _():
            z_copy(z, my_z).start()

        return 0

    def chunk(c, _):
        at_rows = rows_of(c)
        for o in range(1, n_rep):
            grad_copy(c, o, lax.rem(rep + o, n_rep)).wait_recv()

        def hidden_tile(j, _):
            at = pl.ds(pl.multiple_of(j * ff_tile, ff_tile), ff_tile)
            total = jnp.dot(gfull[0, at_rows, :], down_v[:d_own, at],
                            preferred_element_type=jnp.float32)
            for g in range(1, n_rep):
                total += jnp.dot(gfull[g, at_rows, :], down_v[g * d_own:(g + 1) * d_own, at],
                                 preferred_element_type=jnp.float32)
            passed = hid[at_rows, at].astype(jnp.float32) > 0.0
            masked[rep, at_rows, at] = jnp.where(passed, total, 0.0).astype(jnp.bfloat16)
            return 0

        lax.fori_loop(0, ff // ff_tile, hidden_tile, 0)

        for o in range(1, n_rep):
            part_copy(c, o, rep).start()
        if n_rep == 2:
            def own_tile(j, _):
                at = pl.ds(pl.multiple_of(j * d_tile, d_tile), d_tile)
                own_sum[at_rows, at] = jnp.dot(masked[rep, at_rows, :], up_all[rep, :, at],
                                               preferred_element_type=jnp.float32)
                return 0

            lax.fori_loop(0, d_all // d_tile, own_tile, 0)
        return 0

    def spread_start():
        for g in rep_peers:
            landed(g, me)
            over_x(g, my_z).start()
            over_core(g, my_z, my_x).start()
            for o in range(1, n_z):
                over_z(g, lax.rem(my_z + o, n_z)).start()

    def spread_x(o, _):
        z = lax.rem(my_z + o, n_z)
        for g in rep_peers:
            landed(g, index_of(z, my_x, my_c))
            over_x(g, z).start()
            over_core(g, z, my_x).start()
        return 0

    def spread_core(o, _):
        z = lax.rem(my_z + o, n_z)
        for g in rep_peers:
            landed(g, index_of(z, 1 - my_x, my_c))
            over_core(g, z, 1 - my_x).start()
        return 0

    def spread_end(z, _):
        for g in rep_peers:
            for x in range(2):
                landed(g, index_of(z, x, 1 - my_c))
        return 0

    def spread_sent(z, _):
        for g in rep_peers:
            over_x(g, z).wait_send()
            for x in range(2):
                over_core(g, z, x).wait_send()

            @pl.when(z != my_z)
            def _():
                over_z(g, z).wait_send()

        return 0

    lax.fori_loop(0, z_own, make_terms, 0)
    spread_start()
    lax.fori_loop(0, z_own, add_core, 0)
    loads[2].wait()
    loads[3].wait()
    third = max(n_chunks // 3, 1)
    lax.fori_loop(0, third, chunk, 0)
    lax.fori_loop(1, 2, spread_x, 0)
    lax.fori_loop(0, z_own, add_x, 0)
    lax.fori_loop(third, 2 * third, chunk, 0)
    lax.fori_loop(2, n_z, spread_x, 0)
    lax.fori_loop(2 * third, n_chunks, chunk, 0)
    lax.fori_loop(z_own, n_z, make_terms, 0)
    lax.fori_loop(z_own, n_z, add_core, 0)
    lax.fori_loop(0, n_z, spread_core, 0)
    lax.fori_loop(z_own, n_z, add_x, 0)
    lax.fori_loop(0, n_z, spread_end, 0)

    def out_copy(c):
        return pltpu.make_async_copy(obuf.at[rows_of(c)], ig_out.at[rows_of(c)], out_sem.at[c])

    def finish(c, _):
        at_rows = rows_of(c)
        for o in range(1, n_rep):
            part_copy(c, o, lax.rem(rep + o, n_rep)).wait_recv()

        def out_tile(j, _):
            at = pl.ds(pl.multiple_of(j * d_tile, d_tile), d_tile)

            def term(g):
                other_sum[...] = jnp.dot(masked[g, at_rows, :], up_all[g, :, at],
                                         preferred_element_type=jnp.float32)
                return other_sum[...]

            if n_rep == 2:
                total = own_sum[at_rows, at] + term(1 - rep)
            else:
                total = term(0)
                for g in range(1, n_rep):
                    total += term(g)
            obuf[at_rows, at] = total.astype(jnp.bfloat16)
            return 0

        lax.fori_loop(0, d_all // d_tile, out_tile, 0)
        out_copy(c).start()
        return 0

    lax.fori_loop(0, n_chunks // 2, finish, 0)

    total = from_x[my_z].astype(jnp.float32)
    for o in range(1, n_z):
        source = lax.rem(my_z + o, n_z)
        z_copy(source, source).wait()
        total += from_z[source].astype(jnp.float32)
    dg_v[...] = total / n_dp
    dg_copy = pltpu.make_async_copy(dg_v, dg_out, dg_sem)
    dg_copy.start()

    lax.fori_loop(n_chunks // 2, n_chunks, finish, 0)
    for c in range(n_chunks):
        for o in range(1, n_rep):
            grad_copy(c, o, rep).wait_send()
            part_copy(c, o, rep).wait_send()
        out_copy(c).wait()
    for o in range(1, n_rep):
        up_rep_copy(o, rep).wait_send()
    lax.fori_loop(0, n_z, spread_sent, 0)
    dg_copy.wait()


def on_device(n_dp, n_rep, grad_out, pre_act, up_weight, down_weight, slot_counts):
    rows, d_own = grad_out.shape
    ff = pre_act.shape[1]
    d_all = down_weight.shape[0]
    n_z = n_dp // 4
    blk = d_all // n_dp
    n_chunks = rows // CHUNK
    any_ref = pl.BlockSpec(memory_space=pl.ANY)
    bf16, dma = jnp.bfloat16, pltpu.SemaphoreType.DMA
    return pl.pallas_call(
        functools.partial(kernel, n_dp, n_rep),
        out_shape=(jax.ShapeDtypeStruct((rows, d_all), bf16),
                   jax.ShapeDtypeStruct((blk, ff), jnp.float32)),
        in_specs=[pl.BlockSpec(memory_space=pltpu.SMEM)] + [any_ref] * 4,
        out_specs=(any_ref, any_ref),
        scratch_shapes=[
            pltpu.VMEM((n_rep, rows, d_own), bf16),
            pltpu.VMEM((rows, ff), bf16),
            pltpu.VMEM((rows, ff), bf16),
            pltpu.VMEM((n_rep, ff, d_all), bf16),
            pltpu.VMEM((d_all, ff), bf16),
            pltpu.VMEM((n_z, 2, 2, blk, ff), bf16),
            pltpu.VMEM((n_z, 2, blk, ff), bf16),
            pltpu.VMEM((n_z, blk, ff), bf16),
            pltpu.VMEM((n_z, blk, ff), bf16),
            pltpu.VMEM((n_rep, rows, ff), bf16),
            pltpu.VMEM((rows, d_all), jnp.float32),
            pltpu.VMEM((CHUNK, tile_of(d_all)), jnp.float32),
            pltpu.VMEM((rows, d_all), bf16),
            pltpu.VMEM((blk, ff), jnp.float32),
            dma((4,)),
            dma((n_chunks, n_rep)), dma((n_chunks, n_rep)),
            dma((n_chunks, n_rep)), dma((n_chunks, n_rep)),
            dma((n_rep,)), dma((n_rep, n_dp)), dma((n_rep, n_dp)),
            dma((n_z,)), dma((n_z,)), dma((n_z,)), dma((n_z,)), dma((n_z,)), dma((n_z,)),
            dma((n_chunks,)), dma,
        ],
        compiler_params=pltpu.CompilerParams(
            collective_id=0, has_side_effects=True, vmem_limit_bytes=63 * 2**20),
    )(slot_counts, grad_out, pre_act, up_weight, down_weight)


def solution(mesh):
    sizes = dict(mesh.shape)
    return jax.shard_map(
        functools.partial(on_device, sizes["dp"], sizes["rep"]),
        mesh=mesh,
        in_specs=(P("dp", "rep"), P("dp", "rep"), P("rep", None), P(None, "rep"), P("dp")),
        out_specs=(P("dp", None), P("dp", "rep")),
        check_vma=False,
    )
```

```python
import functools

import jax
import jax.numpy as jnp
from jax import lax
from jax.experimental import pallas as pl
from jax.experimental.pallas import tpu as pltpu
from jax.sharding import PartitionSpec as P

MESH = pl.DeviceIdType.MESH
CHUNK = 128


def tile_of(extent):
    return next(t for t in (512, 384, 256, 128) if extent % t == 0)


def kernel(n_dp, n_rep, counts, grad, pre, up, down, ig_out, dg_out,
           gfull, pre_v, hid, up_v, down_v, terms, from_core, from_x, from_z, part, pg,
           load_sem, g_send, g_recv, p_send, p_recv, c_send, c_recv, x_send, x_recv, z_send, z_recv):
    rows, d_own = grad.shape
    ff = pre.shape[1]
    d_all = down.shape[0]
    n_z = n_dp // 4
    z_own = n_z // n_rep
    blk = d_all // n_dp
    n_chunks = rows // CHUNK
    ff_tile, d_tile = tile_of(ff), tile_of(d_all)

    me = lax.axis_index("dp")
    rep = lax.axis_index("rep")
    my_z, my_x, my_c = me // 4, (me // 2) % 2, me % 2
    core_peer = {"dp": my_z * 4 + my_x * 2 + (1 - my_c)}
    x_peer = {"dp": my_z * 4 + (1 - my_x) * 2 + my_c}
    rep_peers = [lax.rem(rep + o, n_rep) for o in range(1, n_rep)]

    def z_peer(z):
        return {"dp": z * 4 + my_x * 2 + my_c}

    loads = [
        pltpu.make_async_copy(src, dst, load_sem.at[i])
        for i, (src, dst) in enumerate(
            ((grad, gfull.at[rep]), (pre, pre_v), (down, down_v), (up, up_v)))
    ]
    for load in loads:
        load.start()

    barrier = pltpu.get_barrier_semaphore()
    peers = [{"rep": r} for r in rep_peers] + [core_peer, x_peer]
    peers += [z_peer(lax.rem(my_z + o, n_z)) for o in range(1, n_z)]
    for peer in peers:
        pl.semaphore_signal(barrier, inc=1, device_id=peer, device_id_type=MESH)
    pl.semaphore_wait(barrier, len(peers))

    def rows_of(c):
        return pl.ds(pl.multiple_of(c * CHUNK, CHUNK), CHUNK)

    def grad_copy(c, o, source):
        return pltpu.make_async_remote_copy(
            src_ref=grad.at[rows_of(c)], dst_ref=gfull.at[source, rows_of(c)],
            send_sem=g_send.at[c, o], recv_sem=g_recv.at[c, source],
            device_id={"rep": lax.rem(rep + o, n_rep)}, device_id_type=MESH)

    def part_copy(c, o, source):
        return pltpu.make_async_remote_copy(
            src_ref=part.at[rep, rows_of(c)], dst_ref=part.at[source, rows_of(c)],
            send_sem=p_send.at[c, o], recv_sem=p_recv.at[c, source],
            device_id={"rep": lax.rem(rep + o, n_rep)}, device_id_type=MESH)

    for c in range(n_chunks):
        for o in range(1, n_rep):
            grad_copy(c, o, rep).start()

    loads[1].wait()
    count = counts[0]

    def mask_rows(c, _):
        at = lax.broadcasted_iota(jnp.int32, (CHUNK, ff), 0) + c * CHUNK
        kept = jnp.where(at < count, pre_v[rows_of(c), :].astype(jnp.float32), 0.0)
        kept = jnp.maximum(kept, 0.0)
        hid[rows_of(c), :] = kept.astype(jnp.bfloat16)
        return 0

    lax.fori_loop(0, n_chunks, mask_rows, 0)
    loads[0].wait()

    def core_copy(z):
        return pltpu.make_async_remote_copy(
            src_ref=terms.at[z, 1 - my_c], dst_ref=from_core.at[z],
            send_sem=c_send.at[z], recv_sem=c_recv.at[z],
            device_id=core_peer, device_id_type=MESH)

    def x_copy(z):
        return pltpu.make_async_remote_copy(
            src_ref=from_core.at[z, 1 - my_x], dst_ref=from_x.at[z],
            send_sem=x_send.at[z], recv_sem=x_recv.at[z],
            device_id=x_peer, device_id_type=MESH)

    def z_copy(z, source):
        return pltpu.make_async_remote_copy(
            src_ref=from_x.at[z], dst_ref=from_z.at[source],
            send_sem=z_send.at[z], recv_sem=z_recv.at[source],
            device_id=z_peer(z), device_id_type=MESH)

    def z_at(k):
        return lax.rem(rep * z_own + k, n_z)

    def make_terms(k, _):
        z = z_at(k)
        group = z // z_own
        cols = pl.ds(pl.multiple_of((z - group * z_own) * 4 * blk, 4 * blk), 4 * blk)

        def one(j, _):
            at = pl.ds(pl.multiple_of(j * ff_tile, ff_tile), ff_tile)
            out = lax.dot_general(
                gfull[group, :, cols], hid[:, at], (((0,), (0,)), ((), ())),
                preferred_element_type=jnp.float32).astype(jnp.bfloat16)
            for x in range(2):
                for core in range(2):
                    row = (x * 2 + core) * blk
                    terms[z, core, x, :, at] = out[row:row + blk]
            return 0

        lax.fori_loop(0, ff // ff_tile, one, 0)
        core_copy(z).start()
        return 0

    def add_core(k, _):
        z = z_at(k)
        core_copy(z).wait()
        for x in range(2):
            total = from_core[z, x].astype(jnp.float32) + terms[z, my_c, x].astype(jnp.float32)
            from_core[z, x] = total.astype(jnp.bfloat16)
        x_copy(z).start()
        return 0

    def add_x(k, _):
        z = z_at(k)
        x_copy(z).wait()
        total = from_x[z].astype(jnp.float32) + from_core[z, my_x].astype(jnp.float32)
        from_x[z] = total.astype(jnp.bfloat16)

        @pl.when(z != my_z)
        def _():
            z_copy(z, my_z).start()

        return 0

    def chunk(c, _):
        at_rows = rows_of(c)
        for o in range(1, n_rep):
            grad_copy(c, o, lax.rem(rep + o, n_rep)).wait_recv()

        def hidden_tile(j, _):
            at = pl.ds(pl.multiple_of(j * ff_tile, ff_tile), ff_tile)
            total = jnp.dot(gfull[0, at_rows, :], down_v[:d_own, at],
                            preferred_element_type=jnp.float32)
            for g in range(1, n_rep):
                total += jnp.dot(gfull[g, at_rows, :], down_v[g * d_own:(g + 1) * d_own, at],
                                 preferred_element_type=jnp.float32)
            passed = hid[at_rows, at].astype(jnp.float32) > 0.0
            pg[:, at] = jnp.where(passed, total, 0.0).astype(jnp.bfloat16)
            return 0

        lax.fori_loop(0, ff // ff_tile, hidden_tile, 0)

        def out_tile(j, _):
            at = pl.ds(pl.multiple_of(j * d_tile, d_tile), d_tile)
            part[rep, at_rows, at] = jnp.dot(
                pg[...], up_v[:, at], preferred_element_type=jnp.float32).astype(jnp.bfloat16)
            return 0

        lax.fori_loop(0, d_all // d_tile, out_tile, 0)
        for o in range(1, n_rep):
            part_copy(c, o, rep).start()
        return 0

    lax.fori_loop(0, z_own, make_terms, 0)
    loads[2].wait()
    loads[3].wait()
    third = max(n_chunks // 3, 1)
    lax.fori_loop(0, third, chunk, 0)
    lax.fori_loop(0, z_own, add_core, 0)
    lax.fori_loop(third, 2 * third, chunk, 0)
    lax.fori_loop(0, z_own, add_x, 0)
    lax.fori_loop(2 * third, n_chunks, chunk, 0)
    lax.fori_loop(z_own, n_z, make_terms, 0)
    lax.fori_loop(z_own, n_z, add_core, 0)
    lax.fori_loop(z_own, n_z, add_x, 0)

    def finish(c, _):
        at_rows = rows_of(c)
        for o in range(1, n_rep):
            part_copy(c, o, lax.rem(rep + o, n_rep)).wait_recv()
        total = part[0, at_rows, :].astype(jnp.float32)
        for g in range(1, n_rep):
            total += part[g, at_rows, :].astype(jnp.float32)
        ig_out[at_rows, :] = total.astype(jnp.bfloat16)
        return 0

    lax.fori_loop(0, n_chunks // 2, finish, 0)

    total = from_x[my_z].astype(jnp.float32)
    for o in range(1, n_z):
        source = lax.rem(my_z + o, n_z)
        z_copy(source, source).wait()
        total += from_z[source].astype(jnp.float32)
    dg_out[...] = total / n_dp

    lax.fori_loop(n_chunks // 2, n_chunks, finish, 0)
    for c in range(n_chunks):
        for o in range(1, n_rep):
            grad_copy(c, o, rep).wait_send()
            part_copy(c, o, rep).wait_send()


def on_device(n_dp, n_rep, grad_out, pre_act, up_weight, down_weight, slot_counts):
    rows, d_own = grad_out.shape
    ff = pre_act.shape[1]
    d_all = down_weight.shape[0]
    n_z = n_dp // 4
    blk = d_all // n_dp
    n_chunks = rows // CHUNK
    any_ref = pl.BlockSpec(memory_space=pl.ANY)
    bf16, dma = jnp.bfloat16, pltpu.SemaphoreType.DMA
    return pl.pallas_call(
        functools.partial(kernel, n_dp, n_rep),
        out_shape=(pltpu.VMEM((rows, d_all), bf16), pltpu.VMEM((blk, ff), jnp.float32)),
        in_specs=[pl.BlockSpec(memory_space=pltpu.SMEM)] + [any_ref] * 4,
        out_specs=(pl.BlockSpec(memory_space=pltpu.VMEM),) * 2,
        scratch_shapes=[
            pltpu.VMEM((n_rep, rows, d_own), bf16),
            pltpu.VMEM((rows, ff), bf16),
            pltpu.VMEM((rows, ff), bf16),
            pltpu.VMEM((ff, d_all), bf16),
            pltpu.VMEM((d_all, ff), bf16),
            pltpu.VMEM((n_z, 2, 2, blk, ff), bf16),
            pltpu.VMEM((n_z, 2, blk, ff), bf16),
            pltpu.VMEM((n_z, blk, ff), bf16),
            pltpu.VMEM((n_z, blk, ff), bf16),
            pltpu.VMEM((n_rep, rows, d_all), bf16),
            pltpu.VMEM((CHUNK, ff), bf16),
            dma((4,)),
            dma((n_chunks, n_rep)), dma((n_chunks, n_rep)),
            dma((n_chunks, n_rep)), dma((n_chunks, n_rep)),
            dma((n_z,)), dma((n_z,)), dma((n_z,)), dma((n_z,)), dma((n_z,)), dma((n_z,)),
        ],
        compiler_params=pltpu.CompilerParams(
            collective_id=0, has_side_effects=True, vmem_limit_bytes=50 * 2**20),
    )(slot_counts, grad_out, pre_act, up_weight, down_weight)


def solution(mesh):
    sizes = dict(mesh.shape)
    return jax.shard_map(
        functools.partial(on_device, sizes["dp"], sizes["rep"]),
        mesh=mesh,
        in_specs=(P("dp", "rep"), P("dp", "rep"), P("rep", None), P(None, "rep"), P("dp")),
        out_specs=(P("dp", None), P("dp", "rep")),
        check_vma=False,
    )
```

```python
import functools

import jax
import jax.numpy as jnp
from jax import lax
from jax.experimental import pallas as pl
from jax.experimental.pallas import tpu as pltpu
from jax.sharding import PartitionSpec as P

MESH = pl.DeviceIdType.MESH
CHUNK = 128


def tile_of(extent):
    return next(t for t in (512, 384, 256, 128) if extent % t == 0)


def kernel(n_dp, n_rep, counts, grad, pre, up, down, ig_out, dg_out,
           gfull, hid, up_all, down_v, terms, from_core, from_x, from_z, masked, own_sum, other_sum,
           load_sem, gp_send, gp_recv, g_send, g_recv, p_send, p_recv, uy_send, u_send, u_recv, c_send, c_recv, x_send, x_recv, z_send, z_recv):
    rows, d_own = grad.shape
    ff = pre.shape[1]
    d_all = down.shape[0]
    n_z = n_dp // 4
    z_own = n_z // n_rep
    blk = d_all // n_dp
    n_chunks = rows // CHUNK
    ff_tile, d_tile = tile_of(ff), tile_of(d_all)
    slice_rows = n_dp
    while ff % (slice_rows * 16):
        slice_rows //= 2
    slice_cols = n_dp // slice_rows
    tall, wide = ff // slice_rows, d_all // slice_cols

    me = lax.axis_index("dp")
    rep = lax.axis_index("rep")
    my_z, my_x, my_c = me // 4, (me // 2) % 2, me % 2
    core_peer = {"dp": my_z * 4 + my_x * 2 + (1 - my_c)}
    x_peer = {"dp": my_z * 4 + (1 - my_x) * 2 + my_c}
    rep_peers = [lax.rem(rep + o, n_rep) for o in range(1, n_rep)]

    def z_peer(z):
        return {"dp": z * 4 + my_x * 2 + my_c}

    loads = [
        pltpu.make_async_copy(src, dst, load_sem.at[i])
        for i, (src, dst) in enumerate(
            ((grad, gfull.at[rep]), (pre, hid), (down, down_v), (up, up_all.at[rep])))
    ]
    for load in loads:
        load.start()

    barrier = pltpu.get_barrier_semaphore()
    peers = [{"rep": r} for r in rep_peers] + [core_peer, x_peer]
    peers += [z_peer(lax.rem(my_z + o, n_z)) for o in range(1, n_z)]
    for peer in peers:
        pl.semaphore_signal(barrier, inc=1, device_id=peer, device_id_type=MESH)
    pl.semaphore_wait(barrier, len(peers))

    def rows_of(c):
        return pl.ds(pl.multiple_of(c * CHUNK, CHUNK), CHUNK)

    last_cols = pl.ds((z_own - 1) * 4 * blk, 4 * blk)

    def grad_copy(c, o, source):
        return pltpu.make_async_remote_copy(
            src_ref=grad.at[rows_of(c), last_cols], dst_ref=gfull.at[source, rows_of(c), last_cols],
            send_sem=g_send.at[c, o], recv_sem=g_recv.at[c, source],
            device_id={"rep": lax.rem(rep + o, n_rep)}, device_id_type=MESH)

    def early_copy(part, o, source):
        cols = pl.ds(part * 4 * blk, 4 * blk)
        return pltpu.make_async_remote_copy(
            src_ref=grad.at[:, cols], dst_ref=gfull.at[source, :, cols],
            send_sem=gp_send.at[o, part], recv_sem=gp_recv.at[source, part],
            device_id={"rep": lax.rem(rep + o, n_rep)}, device_id_type=MESH)

    def part_copy(c, o, source):
        return pltpu.make_async_remote_copy(
            src_ref=masked.at[rep, rows_of(c)], dst_ref=masked.at[source, rows_of(c)],
            send_sem=p_send.at[c, o], recv_sem=p_recv.at[c, source],
            device_id={"rep": lax.rem(rep + o, n_rep)}, device_id_type=MESH)

    def slice_at(s):
        down_at = pl.ds(pl.multiple_of((s // slice_cols) * tall, tall), tall)
        if slice_cols == 1:
            return (down_at,)
        return (down_at, pl.ds(pl.multiple_of((s % slice_cols) * wide, wide), wide))

    def up_rep_copy(o, source):
        return pltpu.make_async_remote_copy(
            src_ref=up.at[slice_at(me)], dst_ref=up_all.at[(source,) + slice_at(me)],
            send_sem=uy_send.at[o], recv_sem=u_recv.at[source, me],
            device_id={"rep": lax.rem(rep + o, n_rep)}, device_id_type=MESH)

    def up_copy(g, s, stage, peer):
        block = up_all.at[(g,) + slice_at(s)]
        return pltpu.make_async_remote_copy(
            src_ref=block, dst_ref=block, send_sem=u_send.at[g, stage], recv_sem=u_recv.at[g, s],
            device_id=peer, device_id_type=MESH)

    def index_of(z, x, core):
        return z * 4 + x * 2 + core

    def over_z(g, z):
        return up_copy(g, me, z, z_peer(z))

    def over_x(g, z):
        return up_copy(g, index_of(z, my_x, my_c), n_z + z, x_peer)

    def over_core(g, z, x):
        return up_copy(g, index_of(z, x, my_c), 2 * n_z + 2 * z + x, core_peer)

    def landed(g, s):
        up_copy(g, s, 0, core_peer).wait_recv()

    for o in range(1, n_rep):
        up_rep_copy(o, rep).start()
    for part in range(z_own - 1):
        for o in range(1, n_rep):
            early_copy(part, o, rep).start()
    for c in range(n_chunks):
        for o in range(1, n_rep):
            grad_copy(c, o, rep).start()

    loads[1].wait()
    count = counts[0]

    def mask_rows(c, _):
        at = lax.broadcasted_iota(jnp.int32, (CHUNK, ff), 0) + c * CHUNK
        kept = jnp.where(at < count, hid[rows_of(c), :].astype(jnp.float32), 0.0)
        kept = jnp.maximum(kept, 0.0)
        hid[rows_of(c), :] = kept.astype(jnp.bfloat16)
        return 0

    lax.fori_loop(0, n_chunks, mask_rows, 0)
    loads[0].wait()

    def core_copy(z):
        return pltpu.make_async_remote_copy(
            src_ref=terms.at[z, 1 - my_c], dst_ref=from_core.at[z],
            send_sem=c_send.at[z], recv_sem=c_recv.at[z],
            device_id=core_peer, device_id_type=MESH)

    def x_copy(z):
        return pltpu.make_async_remote_copy(
            src_ref=from_core.at[z, 1 - my_x], dst_ref=from_x.at[z],
            send_sem=x_send.at[z], recv_sem=x_recv.at[z],
            device_id=x_peer, device_id_type=MESH)

    def z_copy(z, source):
        return pltpu.make_async_remote_copy(
            src_ref=from_x.at[z], dst_ref=from_z.at[source],
            send_sem=z_send.at[z], recv_sem=z_recv.at[source],
            device_id=z_peer(z), device_id_type=MESH)

    def z_at(k):
        late = k - z_own
        other = lax.rem(rep + 1 + lax.rem(late, n_rep - 1), n_rep) * z_own + late // (n_rep - 1)
        return jnp.where(k < z_own, rep * z_own + k, other)

    def make_terms(k, _):
        z = z_at(k)
        group = z // z_own
        cols = pl.ds(pl.multiple_of((z - group * z_own) * 4 * blk, 4 * blk), 4 * blk)

        def one(j, _):
            at = pl.ds(pl.multiple_of(j * ff_tile, ff_tile), ff_tile)
            out = lax.dot_general(
                gfull[group, :, cols], hid[:, at], (((0,), (0,)), ((), ())),
                preferred_element_type=jnp.float32).astype(jnp.bfloat16)
            for x in range(2):
                for core in range(2):
                    row = (x * 2 + core) * blk
                    terms[z, core, x, :, at] = out[row:row + blk]
            return 0

        lax.fori_loop(0, ff // ff_tile, one, 0)
        core_copy(z).start()
        return 0

    def add_core(k, _):
        z = z_at(k)
        core_copy(z).wait()
        for x in range(2):
            total = from_core[z, x].astype(jnp.float32) + terms[z, my_c, x].astype(jnp.float32)
            from_core[z, x] = total.astype(jnp.bfloat16)
        x_copy(z).start()
        return 0

    def add_x(k, _):
        z = z_at(k)
        x_copy(z).wait()
        total = from_x[z].astype(jnp.float32) + from_core[z, my_x].astype(jnp.float32)
        from_x[z] = total.astype(jnp.bfloat16)

        @pl.when(z != my_z)
        def _():
            z_copy(z, my_z).start()

        return 0

    def chunk(c, _):
        at_rows = rows_of(c)
        for o in range(1, n_rep):
            grad_copy(c, o, lax.rem(rep + o, n_rep)).wait_recv()

        def hidden_tile(j, _):
            at = pl.ds(pl.multiple_of(j * ff_tile, ff_tile), ff_tile)
            total = jnp.dot(gfull[0, at_rows, :], down_v[:d_own, at],
                            preferred_element_type=jnp.float32)
            for g in range(1, n_rep):
                total += jnp.dot(gfull[g, at_rows, :], down_v[g * d_own:(g + 1) * d_own, at],
                                 preferred_element_type=jnp.float32)
            passed = hid[at_rows, at].astype(jnp.float32) > 0.0
            masked[rep, at_rows, at] = jnp.where(passed, total, 0.0).astype(jnp.bfloat16)
            return 0

        lax.fori_loop(0, ff // ff_tile, hidden_tile, 0)

        for o in range(1, n_rep):
            part_copy(c, o, rep).start()
        if n_rep == 2:
            def own_tile(j, _):
                at = pl.ds(pl.multiple_of(j * d_tile, d_tile), d_tile)
                own_sum[at_rows, at] = jnp.dot(masked[rep, at_rows, :], up_all[rep, :, at],
                                               preferred_element_type=jnp.float32)
                return 0

            lax.fori_loop(0, d_all // d_tile, own_tile, 0)
        return 0

    def spread_start():
        for g in rep_peers:
            landed(g, me)
            over_x(g, my_z).start()
            over_core(g, my_z, my_x).start()
            for o in range(1, n_z):
                over_z(g, lax.rem(my_z + o, n_z)).start()

    def spread_x(o, _):
        z = lax.rem(my_z + o, n_z)
        for g in rep_peers:
            landed(g, index_of(z, my_x, my_c))
            over_x(g, z).start()
            over_core(g, z, my_x).start()
        return 0

    def spread_core(o, _):
        z = lax.rem(my_z + o, n_z)
        for g in rep_peers:
            landed(g, index_of(z, 1 - my_x, my_c))
            over_core(g, z, 1 - my_x).start()
        return 0

    def spread_end(z, _):
        for g in rep_peers:
            for x in range(2):
                landed(g, index_of(z, x, 1 - my_c))
        return 0

    def spread_sent(z, _):
        for g in rep_peers:
            over_x(g, z).wait_send()
            for x in range(2):
                over_core(g, z, x).wait_send()

            @pl.when(z != my_z)
            def _():
                over_z(g, z).wait_send()

        return 0

    first_late, last_late = z_own, n_z - (n_rep - 1)
    third = max(n_chunks // 3, 1)
    lax.fori_loop(0, z_own, make_terms, 0)
    lax.fori_loop(0, z_own, add_core, 0)
    spread_start()
    for part in range(z_own - 1):
        for o in range(1, n_rep):
            early_copy(part, o, lax.rem(rep + o, n_rep)).wait_recv()
    lax.fori_loop(first_late, last_late, make_terms, 0)
    lax.fori_loop(0, z_own, add_x, 0)
    lax.fori_loop(first_late, last_late, add_core, 0)
    loads[2].wait()
    loads[3].wait()
    lax.fori_loop(0, third, chunk, 0)
    lax.fori_loop(1, 2, spread_x, 0)
    lax.fori_loop(third, 2 * third, chunk, 0)
    lax.fori_loop(first_late, last_late, add_x, 0)
    lax.fori_loop(2 * third, n_chunks, chunk, 0)
    lax.fori_loop(last_late, n_z, make_terms, 0)
    lax.fori_loop(last_late, n_z, add_core, 0)
    lax.fori_loop(2, n_z, spread_x, 0)
    lax.fori_loop(0, 2, spread_core, 0)
    lax.fori_loop(last_late, n_z, add_x, 0)
    lax.fori_loop(2, n_z, spread_core, 0)
    lax.fori_loop(0, n_z, spread_end, 0)

    def finish(c, _):
        at_rows = rows_of(c)
        for o in range(1, n_rep):
            part_copy(c, o, lax.rem(rep + o, n_rep)).wait_recv()

        def out_tile(j, _):
            at = pl.ds(pl.multiple_of(j * d_tile, d_tile), d_tile)

            def term(g):
                other_sum[...] = jnp.dot(masked[g, at_rows, :], up_all[g, :, at],
                                         preferred_element_type=jnp.float32)
                return other_sum[...]

            if n_rep == 2:
                total = own_sum[at_rows, at] + term(1 - rep)
            else:
                total = term(0)
                for g in range(1, n_rep):
                    total += term(g)
            ig_out[at_rows, at] = total.astype(jnp.bfloat16)
            return 0

        lax.fori_loop(0, d_all // d_tile, out_tile, 0)
        return 0

    lax.fori_loop(0, n_chunks // 2, finish, 0)

    total = from_x[my_z].astype(jnp.float32)
    for o in range(1, n_z):
        source = lax.rem(my_z + o, n_z)
        z_copy(source, source).wait()
        total += from_z[source].astype(jnp.float32)
    dg_out[...] = total / n_dp

    lax.fori_loop(n_chunks // 2, n_chunks, finish, 0)
    for c in range(n_chunks):
        for o in range(1, n_rep):
            grad_copy(c, o, rep).wait_send()
            part_copy(c, o, rep).wait_send()
    for part in range(z_own - 1):
        for o in range(1, n_rep):
            early_copy(part, o, rep).wait_send()
    for o in range(1, n_rep):
        up_rep_copy(o, rep).wait_send()
    lax.fori_loop(0, n_z, spread_sent, 0)


def on_device(n_dp, n_rep, grad_out, pre_act, up_weight, down_weight, slot_counts):
    rows, d_own = grad_out.shape
    ff = pre_act.shape[1]
    d_all = down_weight.shape[0]
    n_z = n_dp // 4
    blk = d_all // n_dp
    n_chunks = rows // CHUNK
    any_ref = pl.BlockSpec(memory_space=pl.ANY)
    bf16, dma = jnp.bfloat16, pltpu.SemaphoreType.DMA
    return pl.pallas_call(
        functools.partial(kernel, n_dp, n_rep),
        out_shape=(pltpu.VMEM((rows, d_all), bf16), pltpu.VMEM((blk, ff), jnp.float32)),
        in_specs=[pl.BlockSpec(memory_space=pltpu.SMEM)] + [any_ref] * 4,
        out_specs=(pl.BlockSpec(memory_space=pltpu.VMEM),) * 2,
        scratch_shapes=[
            pltpu.VMEM((n_rep, rows, d_own), bf16),
            pltpu.VMEM((rows, ff), bf16),
            pltpu.VMEM((n_rep, ff, d_all), bf16),
            pltpu.VMEM((d_all, ff), bf16),
            pltpu.VMEM((n_z, 2, 2, blk, ff), bf16),
            pltpu.VMEM((n_z, 2, blk, ff), bf16),
            pltpu.VMEM((n_z, blk, ff), bf16),
            pltpu.VMEM((n_z, blk, ff), bf16),
            pltpu.VMEM((n_rep, rows, ff), bf16),
            pltpu.VMEM((rows, d_all), jnp.float32),
            pltpu.VMEM((CHUNK, tile_of(d_all)), jnp.float32),
            dma((4,)), dma((n_rep, n_z)), dma((n_rep, n_z)),
            dma((n_chunks, n_rep)), dma((n_chunks, n_rep)),
            dma((n_chunks, n_rep)), dma((n_chunks, n_rep)),
            dma((n_rep,)), dma((n_rep, n_dp)), dma((n_rep, n_dp)),
            dma((n_z,)), dma((n_z,)), dma((n_z,)), dma((n_z,)), dma((n_z,)), dma((n_z,)),
        ],
        compiler_params=pltpu.CompilerParams(
            collective_id=0, has_side_effects=True, vmem_limit_bytes=54 * 2**20),
    )(slot_counts, grad_out, pre_act, up_weight, down_weight)


def solution(mesh):
    sizes = dict(mesh.shape)
    return jax.shard_map(
        functools.partial(on_device, sizes["dp"], sizes["rep"]),
        mesh=mesh,
        in_specs=(P("dp", "rep"), P("dp", "rep"), P("rep", None), P(None, "rep"), P("dp")),
        out_specs=(P("dp", None), P("dp", "rep")),
        check_vma=False,
    )
```

```python
import functools

import jax
import jax.numpy as jnp
from jax import lax
from jax.experimental import pallas as pl
from jax.experimental.pallas import tpu as pltpu
from jax.sharding import PartitionSpec as P

MESH = pl.DeviceIdType.MESH
CHUNK = 128


def tile_of(extent):
    return next(t for t in (512, 384, 256, 128) if extent % t == 0)


def kernel(n_dp, n_rep, counts, grad, pre, up, down, ig_out, dg_out,
           gfull, hid, up_all, down_v, terms, from_core, from_x, from_z, masked, own_sum, other_sum,
           load_sem, gp_send, gp_recv, g_send, g_recv, p_send, p_recv, uy_send, u_send, u_recv, c_send, c_recv, x_send, x_recv, z_send, z_recv):
    rows, d_own = grad.shape
    ff = pre.shape[1]
    d_all = down.shape[0]
    n_z = n_dp // 4
    z_own = n_z // n_rep
    blk = d_all // n_dp
    n_chunks = rows // CHUNK
    ff_tile, d_tile = tile_of(ff), tile_of(d_all)
    slice_rows = n_dp
    while ff % (slice_rows * 16):
        slice_rows //= 2
    slice_cols = n_dp // slice_rows
    tall, wide = ff // slice_rows, d_all // slice_cols

    me = lax.axis_index("dp")
    rep = lax.axis_index("rep")
    my_z, my_x, my_c = me // 4, (me // 2) % 2, me % 2
    core_peer = {"dp": my_z * 4 + my_x * 2 + (1 - my_c)}
    x_peer = {"dp": my_z * 4 + (1 - my_x) * 2 + my_c}
    rep_peers = [lax.rem(rep + o, n_rep) for o in range(1, n_rep)]

    def z_peer(z):
        return {"dp": z * 4 + my_x * 2 + my_c}

    loads = [
        pltpu.make_async_copy(src, dst, load_sem.at[i])
        for i, (src, dst) in enumerate(
            ((grad, gfull.at[rep]), (pre, hid), (down, down_v), (up, up_all.at[rep])))
    ]
    for load in loads:
        load.start()

    barrier = pltpu.get_barrier_semaphore()
    peers = [{"rep": r} for r in rep_peers] + [core_peer, x_peer]
    peers += [z_peer(lax.rem(my_z + o, n_z)) for o in range(1, n_z)]
    for peer in peers:
        pl.semaphore_signal(barrier, inc=1, device_id=peer, device_id_type=MESH)
    pl.semaphore_wait(barrier, len(peers))

    def rows_of(c):
        return pl.ds(pl.multiple_of(c * CHUNK, CHUNK), CHUNK)

    last_cols = pl.ds((z_own - 1) * 4 * blk, 4 * blk)

    def grad_copy(c, o, source):
        return pltpu.make_async_remote_copy(
            src_ref=grad.at[rows_of(c), last_cols], dst_ref=gfull.at[source, rows_of(c), last_cols],
            send_sem=g_send.at[c, o], recv_sem=g_recv.at[c, source],
            device_id={"rep": lax.rem(rep + o, n_rep)}, device_id_type=MESH)

    def early_copy(part, o, source):
        cols = pl.ds(part * 4 * blk, 4 * blk)
        return pltpu.make_async_remote_copy(
            src_ref=grad.at[:, cols], dst_ref=gfull.at[source, :, cols],
            send_sem=gp_send.at[o, part], recv_sem=gp_recv.at[source, part],
            device_id={"rep": lax.rem(rep + o, n_rep)}, device_id_type=MESH)

    def part_copy(c, o, source):
        return pltpu.make_async_remote_copy(
            src_ref=masked.at[rep, rows_of(c)], dst_ref=masked.at[source, rows_of(c)],
            send_sem=p_send.at[c, o], recv_sem=p_recv.at[c, source],
            device_id={"rep": lax.rem(rep + o, n_rep)}, device_id_type=MESH)

    def slice_at(s):
        down_at = pl.ds(pl.multiple_of((s // slice_cols) * tall, tall), tall)
        if slice_cols == 1:
            return (down_at,)
        return (down_at, pl.ds(pl.multiple_of((s % slice_cols) * wide, wide), wide))

    def up_rep_copy(o, source):
        return pltpu.make_async_remote_copy(
            src_ref=up.at[slice_at(me)], dst_ref=up_all.at[(source,) + slice_at(me)],
            send_sem=uy_send.at[o], recv_sem=u_recv.at[source, me],
            device_id={"rep": lax.rem(rep + o, n_rep)}, device_id_type=MESH)

    def up_copy(g, s, stage, peer):
        block = up_all.at[(g,) + slice_at(s)]
        return pltpu.make_async_remote_copy(
            src_ref=block, dst_ref=block, send_sem=u_send.at[g, stage], recv_sem=u_recv.at[g, s],
            device_id=peer, device_id_type=MESH)

    def index_of(z, x, core):
        return z * 4 + x * 2 + core

    def along_z(g, z, stage, step):
        to = lax.rem(my_z + step + n_z, n_z)
        return up_copy(g, index_of(z, my_x, my_c), stage, z_peer(to))

    def over_x(g, z):
        return up_copy(g, index_of(z, my_x, my_c), n_z + z, x_peer)

    def over_core(g, z, x):
        return up_copy(g, index_of(z, x, my_c), 2 * n_z + 2 * z + x, core_peer)

    def landed(g, s):
        up_copy(g, s, 0, core_peer).wait_recv()

    for o in range(1, n_rep):
        up_rep_copy(o, rep).start()
    for part in range(z_own - 1):
        for o in range(1, n_rep):
            early_copy(part, o, rep).start()
    for c in range(n_chunks):
        for o in range(1, n_rep):
            grad_copy(c, o, rep).start()

    loads[1].wait()
    count = counts[0]

    def mask_rows(c, _):
        at = lax.broadcasted_iota(jnp.int32, (CHUNK, ff), 0) + c * CHUNK
        kept = jnp.where(at < count, hid[rows_of(c), :].astype(jnp.float32), 0.0)
        kept = jnp.maximum(kept, 0.0)
        hid[rows_of(c), :] = kept.astype(jnp.bfloat16)
        return 0

    lax.fori_loop(0, n_chunks, mask_rows, 0)
    loads[0].wait()

    def core_copy(z):
        return pltpu.make_async_remote_copy(
            src_ref=terms.at[z, 1 - my_c], dst_ref=from_core.at[z],
            send_sem=c_send.at[z], recv_sem=c_recv.at[z],
            device_id=core_peer, device_id_type=MESH)

    def x_copy(z):
        return pltpu.make_async_remote_copy(
            src_ref=from_core.at[z, 1 - my_x], dst_ref=from_x.at[z],
            send_sem=x_send.at[z], recv_sem=x_recv.at[z],
            device_id=x_peer, device_id_type=MESH)

    def z_copy(z, source):
        return pltpu.make_async_remote_copy(
            src_ref=from_x.at[z], dst_ref=from_z.at[source],
            send_sem=z_send.at[z], recv_sem=z_recv.at[source],
            device_id=z_peer(z), device_id_type=MESH)

    def z_at(k):
        late = k - z_own
        other = lax.rem(rep + 1 + lax.rem(late, n_rep - 1), n_rep) * z_own + late // (n_rep - 1)
        return jnp.where(k < z_own, rep * z_own + k, other)

    def make_terms(k, _):
        z = z_at(k)
        group = z // z_own
        cols = pl.ds(pl.multiple_of((z - group * z_own) * 4 * blk, 4 * blk), 4 * blk)

        def one(j, _):
            at = pl.ds(pl.multiple_of(j * ff_tile, ff_tile), ff_tile)
            out = lax.dot_general(
                gfull[group, :, cols], hid[:, at], (((0,), (0,)), ((), ())),
                preferred_element_type=jnp.float32).astype(jnp.bfloat16)
            for x in range(2):
                for core in range(2):
                    row = (x * 2 + core) * blk
                    terms[z, core, x, :, at] = out[row:row + blk]
            return 0

        lax.fori_loop(0, ff // ff_tile, one, 0)
        core_copy(z).start()
        return 0

    def add_core(k, _):
        z = z_at(k)
        core_copy(z).wait()
        for x in range(2):
            total = from_core[z, x].astype(jnp.float32) + terms[z, my_c, x].astype(jnp.float32)
            from_core[z, x] = total.astype(jnp.bfloat16)
        x_copy(z).start()
        return 0

    def add_x(k, _):
        z = z_at(k)
        x_copy(z).wait()
        total = from_x[z].astype(jnp.float32) + from_core[z, my_x].astype(jnp.float32)
        from_x[z] = total.astype(jnp.bfloat16)

        @pl.when(z != my_z)
        def _():
            z_copy(z, my_z).start()

        return 0

    def chunk(c, _):
        at_rows = rows_of(c)
        for o in range(1, n_rep):
            grad_copy(c, o, lax.rem(rep + o, n_rep)).wait_recv()

        def hidden_tile(j, _):
            at = pl.ds(pl.multiple_of(j * ff_tile, ff_tile), ff_tile)
            total = jnp.dot(gfull[0, at_rows, :], down_v[:d_own, at],
                            preferred_element_type=jnp.float32)
            for g in range(1, n_rep):
                total += jnp.dot(gfull[g, at_rows, :], down_v[g * d_own:(g + 1) * d_own, at],
                                 preferred_element_type=jnp.float32)
            passed = hid[at_rows, at].astype(jnp.float32) > 0.0
            masked[rep, at_rows, at] = jnp.where(passed, total, 0.0).astype(jnp.bfloat16)
            return 0

        lax.fori_loop(0, ff // ff_tile, hidden_tile, 0)

        for o in range(1, n_rep):
            part_copy(c, o, rep).start()
        if n_rep == 2:
            def own_tile(j, _):
                at = pl.ds(pl.multiple_of(j * d_tile, d_tile), d_tile)
                own_sum[at_rows, at] = jnp.dot(masked[rep, at_rows, :], up_all[rep, :, at],
                                               preferred_element_type=jnp.float32)
                return 0

            lax.fori_loop(0, d_all // d_tile, own_tile, 0)
        return 0

    def spread_start():
        for g in rep_peers:
            landed(g, me)
            over_x(g, my_z).start()
            over_core(g, my_z, my_x).start()

            @pl.when(my_z + 1 < n_z)
            def _():
                along_z(g, my_z, my_z, 1).start()

            @pl.when(my_z > 0)
            def _():
                along_z(g, my_z, n_dp, -1).start()

    def both_sides(d, visit):
        @pl.when(my_z >= d)
        def _():
            visit(my_z - d, my_z + 1 < n_z, 1)

        @pl.when(my_z + d < n_z)
        def _():
            visit(my_z + d, my_z > 0, -1)

    def spread_x(d, _):
        def visit(z, goes_on, step):
            for g in rep_peers:
                landed(g, index_of(z, my_x, my_c))

                @pl.when(goes_on)
                def _():
                    along_z(g, z, z, step).start()

                over_x(g, z).start()
                over_core(g, z, my_x).start()

        both_sides(d, visit)
        return 0

    def pass_core(z):
        for g in rep_peers:
            landed(g, index_of(z, 1 - my_x, my_c))
            over_core(g, z, 1 - my_x).start()

    def spread_core(d, _):
        both_sides(d, lambda z, goes_on, step: pass_core(z))
        return 0

    def spread_end(z, _):
        for g in rep_peers:
            for x in range(2):
                landed(g, index_of(z, x, 1 - my_c))
        return 0

    def spread_sent(z, _):
        for g in rep_peers:
            over_x(g, z).wait_send()
            for x in range(2):
                over_core(g, z, x).wait_send()

            @pl.when((z <= my_z) & (my_z + 1 < n_z))
            def _():
                along_z(g, z, z, 1).wait_send()

            @pl.when((z > my_z) & (my_z > 0))
            def _():
                along_z(g, z, z, -1).wait_send()

            @pl.when((z == my_z) & (my_z > 0))
            def _():
                along_z(g, z, n_dp, -1).wait_send()

        return 0

    first_late, last_late = z_own, n_z - (n_rep - 1)
    third = max(n_chunks // 3, 1)
    lax.fori_loop(0, z_own, make_terms, 0)
    lax.fori_loop(0, z_own, add_core, 0)
    spread_start()
    for part in range(z_own - 1):
        for o in range(1, n_rep):
            early_copy(part, o, lax.rem(rep + o, n_rep)).wait_recv()
    lax.fori_loop(first_late, last_late, make_terms, 0)
    lax.fori_loop(first_late, last_late, add_core, 0)
    lax.fori_loop(1, 2, spread_x, 0)
    lax.fori_loop(0, z_own, add_x, 0)
    loads[2].wait()
    loads[3].wait()
    lax.fori_loop(0, third, chunk, 0)
    lax.fori_loop(first_late, last_late, add_x, 0)
    lax.fori_loop(third, 2 * third, chunk, 0)
    lax.fori_loop(2, 3, spread_x, 0)
    lax.fori_loop(2 * third, n_chunks, chunk, 0)
    lax.fori_loop(last_late, n_z, make_terms, 0)
    lax.fori_loop(last_late, n_z, add_core, 0)
    lax.fori_loop(3, n_z, spread_x, 0)
    pass_core(my_z)
    lax.fori_loop(1, 2, spread_core, 0)
    lax.fori_loop(last_late, n_z, add_x, 0)
    lax.fori_loop(2, n_z, spread_core, 0)
    lax.fori_loop(0, n_z, spread_end, 0)

    def finish(c, _):
        at_rows = rows_of(c)
        for o in range(1, n_rep):
            part_copy(c, o, lax.rem(rep + o, n_rep)).wait_recv()

        def out_tile(j, _):
            at = pl.ds(pl.multiple_of(j * d_tile, d_tile), d_tile)

            def term(g):
                other_sum[...] = jnp.dot(masked[g, at_rows, :], up_all[g, :, at],
                                         preferred_element_type=jnp.float32)
                return other_sum[...]

            if n_rep == 2:
                total = own_sum[at_rows, at] + term(1 - rep)
            else:
                total = term(0)
                for g in range(1, n_rep):
                    total += term(g)
            ig_out[at_rows, at] = total.astype(jnp.bfloat16)
            return 0

        lax.fori_loop(0, d_all // d_tile, out_tile, 0)
        return 0

    lax.fori_loop(0, n_chunks - 1, finish, 0)

    total = from_x[my_z].astype(jnp.float32)
    for o in range(1, n_z):
        source = lax.rem(my_z + o, n_z)
        z_copy(source, source).wait()
        total += from_z[source].astype(jnp.float32)
    dg_out[...] = total / n_dp

    lax.fori_loop(n_chunks - 1, n_chunks, finish, 0)
    for c in range(n_chunks):
        for o in range(1, n_rep):
            grad_copy(c, o, rep).wait_send()
            part_copy(c, o, rep).wait_send()
    for part in range(z_own - 1):
        for o in range(1, n_rep):
            early_copy(part, o, rep).wait_send()
    for o in range(1, n_rep):
        up_rep_copy(o, rep).wait_send()
    lax.fori_loop(0, n_z, spread_sent, 0)


def on_device(n_dp, n_rep, grad_out, pre_act, up_weight, down_weight, slot_counts):
    rows, d_own = grad_out.shape
    ff = pre_act.shape[1]
    d_all = down_weight.shape[0]
    n_z = n_dp // 4
    blk = d_all // n_dp
    n_chunks = rows // CHUNK
    any_ref = pl.BlockSpec(memory_space=pl.ANY)
    bf16, dma = jnp.bfloat16, pltpu.SemaphoreType.DMA
    return pl.pallas_call(
        functools.partial(kernel, n_dp, n_rep),
        out_shape=(pltpu.VMEM((rows, d_all), bf16), pltpu.VMEM((blk, ff), jnp.float32)),
        in_specs=[pl.BlockSpec(memory_space=pltpu.SMEM)] + [any_ref] * 4,
        out_specs=(pl.BlockSpec(memory_space=pltpu.VMEM),) * 2,
        scratch_shapes=[
            pltpu.VMEM((n_rep, rows, d_own), bf16),
            pltpu.VMEM((rows, ff), bf16),
            pltpu.VMEM((n_rep, ff, d_all), bf16),
            pltpu.VMEM((d_all, ff), bf16),
            pltpu.VMEM((n_z, 2, 2, blk, ff), bf16),
            pltpu.VMEM((n_z, 2, blk, ff), bf16),
            pltpu.VMEM((n_z, blk, ff), bf16),
            pltpu.VMEM((n_z, blk, ff), bf16),
            pltpu.VMEM((n_rep, rows, ff), bf16),
            pltpu.VMEM((rows, d_all), jnp.float32),
            pltpu.VMEM((CHUNK, tile_of(d_all)), jnp.float32),
            dma((4,)), dma((n_rep, n_z)), dma((n_rep, n_z)),
            dma((n_chunks, n_rep)), dma((n_chunks, n_rep)),
            dma((n_chunks, n_rep)), dma((n_chunks, n_rep)),
            dma((n_rep,)), dma((n_rep, n_dp + 1)), dma((n_rep, n_dp)),
            dma((n_z,)), dma((n_z,)), dma((n_z,)), dma((n_z,)), dma((n_z,)), dma((n_z,)),
        ],
        compiler_params=pltpu.CompilerParams(
            collective_id=0, has_side_effects=True, vmem_limit_bytes=54 * 2**20),
    )(slot_counts, grad_out, pre_act, up_weight, down_weight)


def solution(mesh):
    sizes = dict(mesh.shape)
    return jax.shard_map(
        functools.partial(on_device, sizes["dp"], sizes["rep"]),
        mesh=mesh,
        in_specs=(P("dp", "rep"), P("dp", "rep"), P("rep", None), P(None, "rep"), P("dp")),
        out_specs=(P("dp", None), P("dp", "rep")),
        check_vma=False,
    )
```

```python
import functools

import jax
import jax.numpy as jnp
from jax import lax
from jax.experimental import pallas as pl
from jax.experimental.pallas import tpu as pltpu
from jax.sharding import PartitionSpec as P

MESH = pl.DeviceIdType.MESH
CHUNK = 128


def tile_of(extent):
    return next(t for t in (512, 384, 256, 128) if extent % t == 0)


def kernel(n_dp, n_rep, counts, grad, pre, up, down, ig_out, dg_out,
           gfull, hid, up_all, down_v, terms, from_core, from_x, from_z, masked, own_sum, other_sum,
           load_sem, gp_send, gp_recv, g_send, g_recv, p_send, p_recv, uy_send, u_send, u_recv, c_send, c_recv, x_send, x_recv, z_send, z_recv):
    rows, d_own = grad.shape
    ff = pre.shape[1]
    d_all = down.shape[0]
    n_z = n_dp // 4
    z_own = n_z // n_rep
    blk = d_all // n_dp
    n_chunks = rows // CHUNK
    ff_tile, d_tile = tile_of(ff), tile_of(d_all)
    slice_rows = n_dp
    while ff % (slice_rows * 16):
        slice_rows //= 2
    slice_cols = n_dp // slice_rows
    tall, wide = ff // slice_rows, d_all // slice_cols

    me = lax.axis_index("dp")
    rep = lax.axis_index("rep")
    my_z, my_x, my_c = me // 4, (me // 2) % 2, me % 2
    core_peer = {"dp": my_z * 4 + my_x * 2 + (1 - my_c)}
    x_peer = {"dp": my_z * 4 + (1 - my_x) * 2 + my_c}
    rep_peers = [lax.rem(rep + o, n_rep) for o in range(1, n_rep)]

    def z_peer(z):
        return {"dp": z * 4 + my_x * 2 + my_c}

    loads = [
        pltpu.make_async_copy(src, dst, load_sem.at[i])
        for i, (src, dst) in enumerate(
            ((grad, gfull.at[rep]), (pre, hid), (down, down_v), (up, up_all.at[rep])))
    ]
    for load in loads:
        load.start()

    barrier = pltpu.get_barrier_semaphore()
    peers = [{"rep": r} for r in rep_peers] + [core_peer, x_peer]
    peers += [z_peer(lax.rem(my_z + o, n_z)) for o in range(1, n_z)]
    for peer in peers:
        pl.semaphore_signal(barrier, inc=1, device_id=peer, device_id_type=MESH)
    pl.semaphore_wait(barrier, len(peers))

    def rows_of(c):
        return pl.ds(pl.multiple_of(c * CHUNK, CHUNK), CHUNK)

    last_cols = pl.ds((z_own - 1) * 4 * blk, 4 * blk)

    def grad_copy(c, o, source):
        return pltpu.make_async_remote_copy(
            src_ref=grad.at[rows_of(c), last_cols], dst_ref=gfull.at[source, rows_of(c), last_cols],
            send_sem=g_send.at[c, o], recv_sem=g_recv.at[c, source],
            device_id={"rep": lax.rem(rep + o, n_rep)}, device_id_type=MESH)

    def early_copy(part, o, source):
        cols = pl.ds(part * 4 * blk, 4 * blk)
        return pltpu.make_async_remote_copy(
            src_ref=grad.at[:, cols], dst_ref=gfull.at[source, :, cols],
            send_sem=gp_send.at[o, part], recv_sem=gp_recv.at[source, part],
            device_id={"rep": lax.rem(rep + o, n_rep)}, device_id_type=MESH)

    def part_copy(c, o, source):
        return pltpu.make_async_remote_copy(
            src_ref=masked.at[rep, rows_of(c)], dst_ref=masked.at[source, rows_of(c)],
            send_sem=p_send.at[c, o], recv_sem=p_recv.at[c, source],
            device_id={"rep": lax.rem(rep + o, n_rep)}, device_id_type=MESH)

    def slice_at(s):
        down_at = pl.ds(pl.multiple_of((s // slice_cols) * tall, tall), tall)
        if slice_cols == 1:
            return (down_at,)
        return (down_at, pl.ds(pl.multiple_of((s % slice_cols) * wide, wide), wide))

    def up_rep_copy(o, source):
        return pltpu.make_async_remote_copy(
            src_ref=up.at[slice_at(me)], dst_ref=up_all.at[(source,) + slice_at(me)],
            send_sem=uy_send.at[o], recv_sem=u_recv.at[source, me],
            device_id={"rep": lax.rem(rep + o, n_rep)}, device_id_type=MESH)

    def up_copy(g, s, stage, peer):
        block = up_all.at[(g,) + slice_at(s)]
        return pltpu.make_async_remote_copy(
            src_ref=block, dst_ref=block, send_sem=u_send.at[g, stage], recv_sem=u_recv.at[g, s],
            device_id=peer, device_id_type=MESH)

    def index_of(z, x, core):
        return z * 4 + x * 2 + core

    def along_z(g, z, stage, step):
        to = lax.rem(my_z + step + n_z, n_z)
        return up_copy(g, index_of(z, my_x, my_c), stage, z_peer(to))

    def over_x(g, z):
        return up_copy(g, index_of(z, my_x, my_c), n_z + z, x_peer)

    def over_core(g, z, x):
        return up_copy(g, index_of(z, x, my_c), 2 * n_z + 2 * z + x, core_peer)

    def landed(g, s):
        up_copy(g, s, 0, core_peer).wait_recv()

    for o in range(1, n_rep):
        up_rep_copy(o, rep).start()
    for part in range(z_own - 1):
        for o in range(1, n_rep):
            early_copy(part, o, rep).start()
    for c in range(n_chunks):
        for o in range(1, n_rep):
            grad_copy(c, o, rep).start()

    loads[1].wait()
    count = counts[0]

    def mask_rows(c, _):
        at = lax.broadcasted_iota(jnp.int32, (CHUNK, ff), 0) + c * CHUNK
        kept = jnp.where(at < count, hid[rows_of(c), :].astype(jnp.float32), 0.0)
        kept = jnp.maximum(kept, 0.0)
        hid[rows_of(c), :] = kept.astype(jnp.bfloat16)
        return 0

    lax.fori_loop(0, n_chunks, mask_rows, 0)
    loads[0].wait()

    def core_copy(z):
        return pltpu.make_async_remote_copy(
            src_ref=terms.at[z, 1 - my_c], dst_ref=from_core.at[z],
            send_sem=c_send.at[z], recv_sem=c_recv.at[z],
            device_id=core_peer, device_id_type=MESH)

    def x_copy(z):
        return pltpu.make_async_remote_copy(
            src_ref=from_core.at[z, 1 - my_x], dst_ref=from_x.at[z],
            send_sem=x_send.at[z], recv_sem=x_recv.at[z],
            device_id=x_peer, device_id_type=MESH)

    def z_copy(z, source):
        return pltpu.make_async_remote_copy(
            src_ref=from_x.at[z], dst_ref=from_z.at[source],
            send_sem=z_send.at[z], recv_sem=z_recv.at[source],
            device_id=z_peer(z), device_id_type=MESH)

    def z_at(k):
        late = k - z_own
        other = lax.rem(rep + 1 + lax.rem(late, n_rep - 1), n_rep) * z_own + late // (n_rep - 1)
        return jnp.where(k < z_own, rep * z_own + k, other)

    def make_terms(k, _):
        z = z_at(k)
        group = z // z_own
        cols = pl.ds(pl.multiple_of((z - group * z_own) * 4 * blk, 4 * blk), 4 * blk)

        def one(j, _):
            at = pl.ds(pl.multiple_of(j * ff_tile, ff_tile), ff_tile)
            out = lax.dot_general(
                gfull[group, :, cols], hid[:, at], (((0,), (0,)), ((), ())),
                preferred_element_type=jnp.float32).astype(jnp.bfloat16)
            for x in range(2):
                for core in range(2):
                    row = (x * 2 + core) * blk
                    terms[z, core, x, :, at] = out[row:row + blk]
            return 0

        lax.fori_loop(0, ff // ff_tile, one, 0)
        core_copy(z).start()
        return 0

    def add_core(k, _):
        z = z_at(k)
        core_copy(z).wait()
        for x in range(2):
            total = from_core[z, x].astype(jnp.float32) + terms[z, my_c, x].astype(jnp.float32)
            from_core[z, x] = total.astype(jnp.bfloat16)
        x_copy(z).start()
        return 0

    def add_x(k, _):
        z = z_at(k)
        x_copy(z).wait()
        total = from_x[z].astype(jnp.float32) + from_core[z, my_x].astype(jnp.float32)
        from_x[z] = total.astype(jnp.bfloat16)

        @pl.when(z != my_z)
        def _():
            z_copy(z, my_z).start()

        return 0

    def chunk(c, _):
        at_rows = rows_of(c)
        for o in range(1, n_rep):
            grad_copy(c, o, lax.rem(rep + o, n_rep)).wait_recv()

        def hidden_tile(j, _):
            at = pl.ds(pl.multiple_of(j * ff_tile, ff_tile), ff_tile)
            total = jnp.dot(gfull[0, at_rows, :], down_v[:d_own, at],
                            preferred_element_type=jnp.float32)
            for g in range(1, n_rep):
                total += jnp.dot(gfull[g, at_rows, :], down_v[g * d_own:(g + 1) * d_own, at],
                                 preferred_element_type=jnp.float32)
            passed = hid[at_rows, at].astype(jnp.float32) > 0.0
            masked[rep, at_rows, at] = jnp.where(passed, total, 0.0).astype(jnp.bfloat16)
            return 0

        lax.fori_loop(0, ff // ff_tile, hidden_tile, 0)

        for o in range(1, n_rep):
            part_copy(c, o, rep).start()
        if n_rep == 2:
            def own_tile(j, _):
                at = pl.ds(pl.multiple_of(j * d_tile, d_tile), d_tile)
                own_sum[at_rows, at] = jnp.dot(masked[rep, at_rows, :], up_all[rep, :, at],
                                               preferred_element_type=jnp.float32)
                return 0

            lax.fori_loop(0, d_all // d_tile, own_tile, 0)
        return 0

    def spread_start():
        for g in rep_peers:
            landed(g, me)
            over_x(g, my_z).start()
            over_core(g, my_z, my_x).start()

            @pl.when(my_z + 1 < n_z)
            def _():
                along_z(g, my_z, my_z, 1).start()

            @pl.when(my_z > 0)
            def _():
                along_z(g, my_z, n_dp, -1).start()

    def both_sides(d, visit):
        @pl.when(my_z >= d)
        def _():
            visit(my_z - d, my_z + 1 < n_z, 1)

        @pl.when(my_z + d < n_z)
        def _():
            visit(my_z + d, my_z > 0, -1)

    def spread_z(d, _):
        def visit(z, goes_on, step):
            for g in rep_peers:
                landed(g, index_of(z, my_x, my_c))

                @pl.when(goes_on)
                def _():
                    along_z(g, z, z, step).start()

                over_core(g, z, my_x).start()

        both_sides(d, visit)
        return 0

    def cross_x(d, _):
        def visit(z, goes_on, step):
            for g in rep_peers:
                over_x(g, z).start()

        both_sides(d, visit)
        return 0

    def pass_core(z):
        for g in rep_peers:
            landed(g, index_of(z, 1 - my_x, my_c))
            over_core(g, z, 1 - my_x).start()

    def spread_core(d, _):
        both_sides(d, lambda z, goes_on, step: pass_core(z))
        return 0

    def spread_end(z, _):
        for g in rep_peers:
            for x in range(2):
                landed(g, index_of(z, x, 1 - my_c))
        return 0

    def spread_sent(z, _):
        for g in rep_peers:
            over_x(g, z).wait_send()
            for x in range(2):
                over_core(g, z, x).wait_send()

            @pl.when((z <= my_z) & (my_z + 1 < n_z))
            def _():
                along_z(g, z, z, 1).wait_send()

            @pl.when((z > my_z) & (my_z > 0))
            def _():
                along_z(g, z, z, -1).wait_send()

            @pl.when((z == my_z) & (my_z > 0))
            def _():
                along_z(g, z, n_dp, -1).wait_send()

        return 0

    first_late, last_late = z_own, n_z - (n_rep - 1)
    third = max(n_chunks // 3, 1)
    lax.fori_loop(0, z_own, make_terms, 0)
    lax.fori_loop(0, z_own, add_core, 0)
    spread_start()
    for part in range(z_own - 1):
        for o in range(1, n_rep):
            early_copy(part, o, lax.rem(rep + o, n_rep)).wait_recv()
    lax.fori_loop(first_late, last_late, make_terms, 0)
    lax.fori_loop(first_late, last_late, add_core, 0)
    lax.fori_loop(1, 2, spread_z, 0)
    lax.fori_loop(1, 2, cross_x, 0)
    lax.fori_loop(0, z_own, add_x, 0)
    loads[2].wait()
    loads[3].wait()
    lax.fori_loop(0, third, chunk, 0)
    lax.fori_loop(first_late, last_late, add_x, 0)
    lax.fori_loop(third, 2 * third, chunk, 0)
    lax.fori_loop(2, 3, spread_z, 0)
    lax.fori_loop(2 * third, n_chunks, chunk, 0)
    lax.fori_loop(last_late, n_z, make_terms, 0)
    lax.fori_loop(last_late, n_z, add_core, 0)
    lax.fori_loop(2, 3, cross_x, 0)
    lax.fori_loop(3, n_z, spread_z, 0)
    lax.fori_loop(3, n_z, cross_x, 0)
    pass_core(my_z)
    lax.fori_loop(1, 2, spread_core, 0)
    lax.fori_loop(last_late, n_z, add_x, 0)
    lax.fori_loop(2, n_z, spread_core, 0)
    lax.fori_loop(0, n_z, spread_end, 0)

    def finish(c, _):
        at_rows = rows_of(c)
        for o in range(1, n_rep):
            part_copy(c, o, lax.rem(rep + o, n_rep)).wait_recv()

        def out_tile(j, _):
            at = pl.ds(pl.multiple_of(j * d_tile, d_tile), d_tile)

            def term(g):
                other_sum[...] = jnp.dot(masked[g, at_rows, :], up_all[g, :, at],
                                         preferred_element_type=jnp.float32)
                return other_sum[...]

            if n_rep == 2:
                total = own_sum[at_rows, at] + term(1 - rep)
            else:
                total = term(0)
                for g in range(1, n_rep):
                    total += term(g)
            ig_out[at_rows, at] = total.astype(jnp.bfloat16)
            return 0

        lax.fori_loop(0, d_all // d_tile, out_tile, 0)
        return 0

    lax.fori_loop(0, n_chunks - 1, finish, 0)

    total = from_x[my_z].astype(jnp.float32)
    for o in range(1, n_z):
        source = lax.rem(my_z + o, n_z)
        z_copy(source, source).wait()
        total += from_z[source].astype(jnp.float32)
    dg_out[...] = total / n_dp

    lax.fori_loop(n_chunks - 1, n_chunks, finish, 0)
    for c in range(n_chunks):
        for o in range(1, n_rep):
            grad_copy(c, o, rep).wait_send()
            part_copy(c, o, rep).wait_send()
    for part in range(z_own - 1):
        for o in range(1, n_rep):
            early_copy(part, o, rep).wait_send()
    for o in range(1, n_rep):
        up_rep_copy(o, rep).wait_send()
    lax.fori_loop(0, n_z, spread_sent, 0)


def on_device(n_dp, n_rep, grad_out, pre_act, up_weight, down_weight, slot_counts):
    rows, d_own = grad_out.shape
    ff = pre_act.shape[1]
    d_all = down_weight.shape[0]
    n_z = n_dp // 4
    blk = d_all // n_dp
    n_chunks = rows // CHUNK
    any_ref = pl.BlockSpec(memory_space=pl.ANY)
    bf16, dma = jnp.bfloat16, pltpu.SemaphoreType.DMA
    return pl.pallas_call(
        functools.partial(kernel, n_dp, n_rep),
        out_shape=(pltpu.VMEM((rows, d_all), bf16), pltpu.VMEM((blk, ff), jnp.float32)),
        in_specs=[pl.BlockSpec(memory_space=pltpu.SMEM)] + [any_ref] * 4,
        out_specs=(pl.BlockSpec(memory_space=pltpu.VMEM),) * 2,
        scratch_shapes=[
            pltpu.VMEM((n_rep, rows, d_own), bf16),
            pltpu.VMEM((rows, ff), bf16),
            pltpu.VMEM((n_rep, ff, d_all), bf16),
            pltpu.VMEM((d_all, ff), bf16),
            pltpu.VMEM((n_z, 2, 2, blk, ff), bf16),
            pltpu.VMEM((n_z, 2, blk, ff), bf16),
            pltpu.VMEM((n_z, blk, ff), bf16),
            pltpu.VMEM((n_z, blk, ff), bf16),
            pltpu.VMEM((n_rep, rows, ff), bf16),
            pltpu.VMEM((rows, d_all), jnp.float32),
            pltpu.VMEM((CHUNK, tile_of(d_all)), jnp.float32),
            dma((4,)), dma((n_rep, n_z)), dma((n_rep, n_z)),
            dma((n_chunks, n_rep)), dma((n_chunks, n_rep)),
            dma((n_chunks, n_rep)), dma((n_chunks, n_rep)),
            dma((n_rep,)), dma((n_rep, n_dp + 1)), dma((n_rep, n_dp)),
            dma((n_z,)), dma((n_z,)), dma((n_z,)), dma((n_z,)), dma((n_z,)), dma((n_z,)),
        ],
        compiler_params=pltpu.CompilerParams(
            collective_id=0, has_side_effects=True, vmem_limit_bytes=54 * 2**20),
    )(slot_counts, grad_out, pre_act, up_weight, down_weight)


def solution(mesh):
    sizes = dict(mesh.shape)
    return jax.shard_map(
        functools.partial(on_device, sizes["dp"], sizes["rep"]),
        mesh=mesh,
        in_specs=(P("dp", "rep"), P("dp", "rep"), P("rep", None), P(None, "rep"), P("dp")),
        out_specs=(P("dp", None), P("dp", "rep")),
        check_vma=False,
    )
```

```python
import functools

import jax
import jax.numpy as jnp
from jax import lax
from jax.experimental import pallas as pl
from jax.experimental.pallas import tpu as pltpu
from jax.sharding import PartitionSpec as P

MESH = pl.DeviceIdType.MESH
CHUNK = 128


def tile_of(extent):
    return next(t for t in (512, 384, 256, 128) if extent % t == 0)


def kernel(n_dp, n_rep, counts, grad, pre, up, down, ig_out, dg_out,
           gfull, hid, up_all, down_v, terms, from_core, from_x, from_z, masked, own_sum, other_sum,
           load_sem, gp_send, gp_recv, g_send, g_recv, p_send, p_recv, uy_send, u_send, u_recv, c_send, c_recv, x_send, x_recv, z_send, z_recv):
    rows, d_own = grad.shape
    ff = pre.shape[1]
    d_all = down.shape[0]
    n_z = n_dp // 4
    z_own = n_z // n_rep
    blk = d_all // n_dp
    n_chunks = rows // CHUNK
    ff_tile, d_tile = tile_of(ff), tile_of(d_all)
    slice_rows = n_dp
    while ff % (slice_rows * 16):
        slice_rows //= 2
    slice_cols = n_dp // slice_rows
    tall, wide = ff // slice_rows, d_all // slice_cols

    me = lax.axis_index("dp")
    rep = lax.axis_index("rep")
    my_z, my_x, my_c = me // 4, (me // 2) % 2, me % 2
    core_peer = {"dp": my_z * 4 + my_x * 2 + (1 - my_c)}
    x_peer = {"dp": my_z * 4 + (1 - my_x) * 2 + my_c}
    rep_peers = [lax.rem(rep + o, n_rep) for o in range(1, n_rep)]

    def z_peer(z):
        return {"dp": z * 4 + my_x * 2 + my_c}

    loads = [
        pltpu.make_async_copy(src, dst, load_sem.at[i])
        for i, (src, dst) in enumerate(
            ((grad, gfull.at[rep]), (pre, hid), (down, down_v), (up, up_all.at[rep])))
    ]
    for load in loads:
        load.start()

    barrier = pltpu.get_barrier_semaphore()
    peers = [{"rep": r} for r in rep_peers] + [core_peer, x_peer]
    peers += [z_peer(lax.rem(my_z + o, n_z)) for o in range(1, n_z)]
    for peer in peers:
        pl.semaphore_signal(barrier, inc=1, device_id=peer, device_id_type=MESH)
    pl.semaphore_wait(barrier, len(peers))

    def rows_of(c):
        return pl.ds(pl.multiple_of(c * CHUNK, CHUNK), CHUNK)

    last_cols = pl.ds((z_own - 1) * 4 * blk, 4 * blk)

    def grad_copy(c, o, source):
        return pltpu.make_async_remote_copy(
            src_ref=grad.at[rows_of(c), last_cols], dst_ref=gfull.at[source, rows_of(c), last_cols],
            send_sem=g_send.at[c, o], recv_sem=g_recv.at[c, source],
            device_id={"rep": lax.rem(rep + o, n_rep)}, device_id_type=MESH)

    def early_copy(part, o, source):
        cols = pl.ds(part * 4 * blk, 4 * blk)
        return pltpu.make_async_remote_copy(
            src_ref=grad.at[:, cols], dst_ref=gfull.at[source, :, cols],
            send_sem=gp_send.at[o, part], recv_sem=gp_recv.at[source, part],
            device_id={"rep": lax.rem(rep + o, n_rep)}, device_id_type=MESH)

    def part_copy(c, o, source):
        return pltpu.make_async_remote_copy(
            src_ref=masked.at[rep, rows_of(c)], dst_ref=masked.at[source, rows_of(c)],
            send_sem=p_send.at[c, o], recv_sem=p_recv.at[c, source],
            device_id={"rep": lax.rem(rep + o, n_rep)}, device_id_type=MESH)

    def slice_at(s):
        down_at = pl.ds(pl.multiple_of((s // slice_cols) * tall, tall), tall)
        if slice_cols == 1:
            return (down_at,)
        return (down_at, pl.ds(pl.multiple_of((s % slice_cols) * wide, wide), wide))

    def up_rep_copy(o, source):
        return pltpu.make_async_remote_copy(
            src_ref=up.at[slice_at(me)], dst_ref=up_all.at[(source,) + slice_at(me)],
            send_sem=uy_send.at[o], recv_sem=u_recv.at[source, me],
            device_id={"rep": lax.rem(rep + o, n_rep)}, device_id_type=MESH)

    def up_copy(g, s, stage, peer):
        block = up_all.at[(g,) + slice_at(s)]
        return pltpu.make_async_remote_copy(
            src_ref=block, dst_ref=block, send_sem=u_send.at[g, stage], recv_sem=u_recv.at[g, s],
            device_id=peer, device_id_type=MESH)

    def index_of(z, x, core):
        return z * 4 + x * 2 + core

    def along_z(g, z, stage, step):
        to = lax.rem(my_z + step + n_z, n_z)
        return up_copy(g, index_of(z, my_x, my_c), stage, z_peer(to))

    def over_x(g, z):
        return up_copy(g, index_of(z, my_x, my_c), n_z + z, x_peer)

    def over_core(g, z, x):
        return up_copy(g, index_of(z, x, my_c), 2 * n_z + 2 * z + x, core_peer)

    def landed(g, s):
        up_copy(g, s, 0, core_peer).wait_recv()

    for o in range(1, n_rep):
        up_rep_copy(o, rep).start()
    for part in range(z_own - 1):
        for o in range(1, n_rep):
            early_copy(part, o, rep).start()
    for c in range(n_chunks):
        for o in range(1, n_rep):
            grad_copy(c, o, rep).start()

    loads[1].wait()
    count = counts[0]

    def mask_rows(c, _):
        at = lax.broadcasted_iota(jnp.int32, (CHUNK, ff), 0) + c * CHUNK
        kept = jnp.where(at < count, hid[rows_of(c), :].astype(jnp.float32), 0.0)
        kept = jnp.maximum(kept, 0.0)
        hid[rows_of(c), :] = kept.astype(jnp.bfloat16)
        return 0

    lax.fori_loop(0, n_chunks, mask_rows, 0)
    loads[0].wait()

    def core_copy(z):
        return pltpu.make_async_remote_copy(
            src_ref=terms.at[z, 1 - my_c], dst_ref=from_core.at[z],
            send_sem=c_send.at[z], recv_sem=c_recv.at[z],
            device_id=core_peer, device_id_type=MESH)

    def x_copy(z):
        return pltpu.make_async_remote_copy(
            src_ref=from_core.at[z, 1 - my_x], dst_ref=from_x.at[z],
            send_sem=x_send.at[z], recv_sem=x_recv.at[z],
            device_id=x_peer, device_id_type=MESH)

    def z_copy(z, source):
        return pltpu.make_async_remote_copy(
            src_ref=from_x.at[z], dst_ref=from_z.at[source],
            send_sem=z_send.at[z], recv_sem=z_recv.at[source],
            device_id=z_peer(z), device_id_type=MESH)

    def z_at(k):
        late = k - z_own
        other = lax.rem(rep + 1 + lax.rem(late, n_rep - 1), n_rep) * z_own + late // (n_rep - 1)
        return jnp.where(k < z_own, rep * z_own + k, other)

    def make_terms(k, _):
        z = z_at(k)
        group = z // z_own
        cols = pl.ds(pl.multiple_of((z - group * z_own) * 4 * blk, 4 * blk), 4 * blk)

        def one(j, _):
            at = pl.ds(pl.multiple_of(j * ff_tile, ff_tile), ff_tile)
            out = lax.dot_general(
                gfull[group, :, cols], hid[:, at], (((0,), (0,)), ((), ())),
                preferred_element_type=jnp.float32).astype(jnp.bfloat16)
            for x in range(2):
                for core in range(2):
                    row = (x * 2 + core) * blk
                    terms[z, core, x, :, at] = out[row:row + blk]
            return 0

        lax.fori_loop(0, ff // ff_tile, one, 0)
        core_copy(z).start()
        return 0

    def add_core(k, _):
        z = z_at(k)
        core_copy(z).wait()
        for x in range(2):
            total = from_core[z, x].astype(jnp.float32) + terms[z, my_c, x].astype(jnp.float32)
            from_core[z, x] = total.astype(jnp.bfloat16)
        x_copy(z).start()
        return 0

    def add_x(k, _):
        z = z_at(k)
        x_copy(z).wait()
        total = from_x[z].astype(jnp.float32) + from_core[z, my_x].astype(jnp.float32)
        from_x[z] = total.astype(jnp.bfloat16)

        @pl.when(z != my_z)
        def _():
            z_copy(z, my_z).start()

        return 0

    def chunk(c, _):
        at_rows = rows_of(c)
        for o in range(1, n_rep):
            grad_copy(c, o, lax.rem(rep + o, n_rep)).wait_recv()

        def hidden_tile(j, _):
            at = pl.ds(pl.multiple_of(j * ff_tile, ff_tile), ff_tile)
            total = jnp.dot(gfull[0, at_rows, :], down_v[:d_own, at],
                            preferred_element_type=jnp.float32)
            for g in range(1, n_rep):
                total += jnp.dot(gfull[g, at_rows, :], down_v[g * d_own:(g + 1) * d_own, at],
                                 preferred_element_type=jnp.float32)
            passed = hid[at_rows, at].astype(jnp.float32) > 0.0
            masked[rep, at_rows, at] = jnp.where(passed, total, 0.0).astype(jnp.bfloat16)
            return 0

        lax.fori_loop(0, ff // ff_tile, hidden_tile, 0)

        for o in range(1, n_rep):
            part_copy(c, o, rep).start()
        if n_rep == 2:
            def own_tile(j, _):
                at = pl.ds(pl.multiple_of(j * d_tile, d_tile), d_tile)
                own_sum[at_rows, at] = jnp.dot(masked[rep, at_rows, :], up_all[rep, :, at],
                                               preferred_element_type=jnp.float32)
                return 0

            lax.fori_loop(0, d_all // d_tile, own_tile, 0)
        return 0

    def spread_start():
        for g in rep_peers:
            landed(g, me)
            over_x(g, my_z).start()
            over_core(g, my_z, my_x).start()

            @pl.when(my_z + 1 < n_z)
            def _():
                along_z(g, my_z, my_z, 1).start()

            @pl.when(my_z > 0)
            def _():
                along_z(g, my_z, n_dp, -1).start()

    def both_sides(d, visit):
        @pl.when(my_z >= d)
        def _():
            visit(my_z - d, my_z + 1 < n_z, 1)

        @pl.when(my_z + d < n_z)
        def _():
            visit(my_z + d, my_z > 0, -1)

    def spread_z(d, _):
        def visit(z, goes_on, step):
            for g in rep_peers:
                landed(g, index_of(z, my_x, my_c))

                @pl.when(goes_on)
                def _():
                    along_z(g, z, z, step).start()

                over_core(g, z, my_x).start()

        both_sides(d, visit)
        return 0

    def cross_x(d, _):
        def visit(z, goes_on, step):
            for g in rep_peers:
                over_x(g, z).start()

        both_sides(d, visit)
        return 0

    def pass_core(z):
        for g in rep_peers:
            landed(g, index_of(z, 1 - my_x, my_c))
            over_core(g, z, 1 - my_x).start()

    def spread_core(d, _):
        both_sides(d, lambda z, goes_on, step: pass_core(z))
        return 0

    def spread_end(z, _):
        for g in rep_peers:
            for x in range(2):
                landed(g, index_of(z, x, 1 - my_c))
        return 0

    def spread_sent(z, _):
        for g in rep_peers:
            over_x(g, z).wait_send()
            for x in range(2):
                over_core(g, z, x).wait_send()

            @pl.when((z <= my_z) & (my_z + 1 < n_z))
            def _():
                along_z(g, z, z, 1).wait_send()

            @pl.when((z > my_z) & (my_z > 0))
            def _():
                along_z(g, z, z, -1).wait_send()

            @pl.when((z == my_z) & (my_z > 0))
            def _():
                along_z(g, z, n_dp, -1).wait_send()

        return 0

    first_late, last_late = z_own, n_z - (n_rep - 1)
    third = max(n_chunks // 3, 1)
    lax.fori_loop(0, z_own, make_terms, 0)
    lax.fori_loop(0, z_own, add_core, 0)
    spread_start()
    for part in range(z_own - 1):
        for o in range(1, n_rep):
            early_copy(part, o, lax.rem(rep + o, n_rep)).wait_recv()
    lax.fori_loop(first_late, last_late, make_terms, 0)
    lax.fori_loop(first_late, last_late, add_core, 0)
    lax.fori_loop(1, 2, spread_z, 0)
    lax.fori_loop(1, 2, cross_x, 0)
    lax.fori_loop(0, z_own, add_x, 0)
    loads[2].wait()
    loads[3].wait()
    lax.fori_loop(0, third, chunk, 0)
    lax.fori_loop(first_late, last_late, add_x, 0)
    lax.fori_loop(third, 2 * third, chunk, 0)
    lax.fori_loop(2, 3, spread_z, 0)
    lax.fori_loop(2 * third, n_chunks, chunk, 0)
    lax.fori_loop(last_late, n_z, make_terms, 0)
    lax.fori_loop(last_late, n_z, add_core, 0)
    lax.fori_loop(2, 3, cross_x, 0)
    lax.fori_loop(last_late, n_z, add_x, 0)
    lax.fori_loop(3, n_z, spread_z, 0)
    lax.fori_loop(3, n_z, cross_x, 0)
    pass_core(my_z)
    lax.fori_loop(1, 2, spread_core, 0)
    lax.fori_loop(2, n_z, spread_core, 0)
    lax.fori_loop(0, n_z, spread_end, 0)

    def finish(c, _):
        at_rows = rows_of(c)
        for o in range(1, n_rep):
            part_copy(c, o, lax.rem(rep + o, n_rep)).wait_recv()

        def out_tile(j, _):
            at = pl.ds(pl.multiple_of(j * d_tile, d_tile), d_tile)

            def term(g):
                other_sum[...] = jnp.dot(masked[g, at_rows, :], up_all[g, :, at],
                                         preferred_element_type=jnp.float32)
                return other_sum[...]

            if n_rep == 2:
                total = own_sum[at_rows, at] + term(1 - rep)
            else:
                total = term(0)
                for g in range(1, n_rep):
                    total += term(g)
            ig_out[at_rows, at] = total.astype(jnp.bfloat16)
            return 0

        lax.fori_loop(0, d_all // d_tile, out_tile, 0)
        return 0

    lax.fori_loop(0, n_chunks - 1, finish, 0)

    total = from_x[my_z].astype(jnp.float32)
    for o in range(1, n_z):
        source = lax.rem(my_z + o, n_z)
        z_copy(source, source).wait()
        total += from_z[source].astype(jnp.float32)
    dg_out[...] = total / n_dp

    lax.fori_loop(n_chunks - 1, n_chunks, finish, 0)
    for c in range(n_chunks):
        for o in range(1, n_rep):
            grad_copy(c, o, rep).wait_send()
            part_copy(c, o, rep).wait_send()
    for part in range(z_own - 1):
        for o in range(1, n_rep):
            early_copy(part, o, rep).wait_send()
    for o in range(1, n_rep):
        up_rep_copy(o, rep).wait_send()
    lax.fori_loop(0, n_z, spread_sent, 0)


def on_device(n_dp, n_rep, grad_out, pre_act, up_weight, down_weight, slot_counts):
    rows, d_own = grad_out.shape
    ff = pre_act.shape[1]
    d_all = down_weight.shape[0]
    n_z = n_dp // 4
    blk = d_all // n_dp
    n_chunks = rows // CHUNK
    any_ref = pl.BlockSpec(memory_space=pl.ANY)
    bf16, dma = jnp.bfloat16, pltpu.SemaphoreType.DMA
    return pl.pallas_call(
        functools.partial(kernel, n_dp, n_rep),
        out_shape=(pltpu.VMEM((rows, d_all), bf16), pltpu.VMEM((blk, ff), jnp.float32)),
        in_specs=[pl.BlockSpec(memory_space=pltpu.SMEM)] + [any_ref] * 4,
        out_specs=(pl.BlockSpec(memory_space=pltpu.VMEM),) * 2,
        scratch_shapes=[
            pltpu.VMEM((n_rep, rows, d_own), bf16),
            pltpu.VMEM((rows, ff), bf16),
            pltpu.VMEM((n_rep, ff, d_all), bf16),
            pltpu.VMEM((d_all, ff), bf16),
            pltpu.VMEM((n_z, 2, 2, blk, ff), bf16),
            pltpu.VMEM((n_z, 2, blk, ff), bf16),
            pltpu.VMEM((n_z, blk, ff), bf16),
            pltpu.VMEM((n_z, blk, ff), bf16),
            pltpu.VMEM((n_rep, rows, ff), bf16),
            pltpu.VMEM((rows, d_all), jnp.float32),
            pltpu.VMEM((CHUNK, tile_of(d_all)), jnp.float32),
            dma((4,)), dma((n_rep, n_z)), dma((n_rep, n_z)),
            dma((n_chunks, n_rep)), dma((n_chunks, n_rep)),
            dma((n_chunks, n_rep)), dma((n_chunks, n_rep)),
            dma((n_rep,)), dma((n_rep, n_dp + 1)), dma((n_rep, n_dp)),
            dma((n_z,)), dma((n_z,)), dma((n_z,)), dma((n_z,)), dma((n_z,)), dma((n_z,)),
        ],
        compiler_params=pltpu.CompilerParams(
            collective_id=0, has_side_effects=True, vmem_limit_bytes=54 * 2**20),
    )(slot_counts, grad_out, pre_act, up_weight, down_weight)


def solution(mesh):
    sizes = dict(mesh.shape)
    return jax.shard_map(
        functools.partial(on_device, sizes["dp"], sizes["rep"]),
        mesh=mesh,
        in_specs=(P("dp", "rep"), P("dp", "rep"), P("rep", None), P(None, "rep"), P("dp")),
        out_specs=(P("dp", None), P("dp", "rep")),
        check_vma=False,
    )
```
